256 devices in a mesh: dp: 8 (over z_lo, x), seq: 32 (over y, z_hi, core).
Axes of the slice: x: 4, y: 4, z: 8 (z_hi: 4, z_lo: 2; z = z_hi * 2 + z_lo), core: 2. Of those that a mesh axis runs over, the one named last changes fastest.
Arguments:
- queries: bfloat16 [8, 4096, 4096], P('dp', 'seq'), may hold values from -5 to 5
- rotated_key_rows: bfloat16 [8, 4096, 512], P('dp', 'seq'), may hold values from -5 to 5
- hidden_states: bfloat16 [8, 4096, 8192], P('dp', 'seq'), may hold values from -6 to 6
- block_order: int32 [64], replicated, may hold values from 0 to 63, each once
- first_weight: bfloat16 [8192, 512], replicated, may hold values from -0.0625 to 0.0625
- first_bias: float32 [512], replicated, may hold values from -3 to 3
- output_weight: bfloat16 [4, 512], replicated, may hold values from -0.25 to 0.25
- output_bias: float32 [4], replicated, may hold values from -1 to 1
Outputs:
- token_attention_mass: float32 [8, 4, 4096], P('dp', None, 'seq')
- loss_value: float32 [], replicated
- step_first: float32 [8192, 512], P('seq')
- output_weight_step: float32 [4, 512], replicated
- step_bias: float32 [512], replicated
- grad_bias: float32 [4], replicated
The draws below stay inside these ranges and needn't reach their ends.
All inputs are finite; a program needn't handle non-finite values.
Results may differ from the reference program's by a relative error of at most 0.0023.
Values may be sent and summed in bfloat16 or wider, within the bound.
A program may use at most 64 MiB of HBM per device.

```python
import math
import jax
import jax.numpy as jnp
from jax import lax

D = 8192
HQ = 32
KEY_VALUE_HEADS = 4
HEAD_SIZE = 128
RETAIN_HIDDEN = 512
BLK = 64
QUERY_GROUP_SIZE = 8
SEQUENCE_LENGTH = 4096
BLOCKS = 64
SEQUENCE_COUNT = 8


def draw_queries(key, part):
    value_rows = jnp.clip(0.3 * jax.random.normal(jax.random.fold_in(key, 31), (SEQUENCE_COUNT, SEQUENCE_LENGTH, KEY_VALUE_HEADS, QUERY_GROUP_SIZE, HEAD_SIZE)), -5.0, 5.0)
    return value_rows.reshape(SEQUENCE_COUNT, SEQUENCE_LENGTH, HQ * HEAD_SIZE).astype(jnp.bfloat16)


def draw_rotated_key_rows(key, part):
    value_rows = jnp.clip(0.3 * jax.random.normal(jax.random.fold_in(key, 32), (SEQUENCE_COUNT, SEQUENCE_LENGTH, KEY_VALUE_HEADS, HEAD_SIZE)), -5.0, 5.0)
    return value_rows.reshape(SEQUENCE_COUNT, SEQUENCE_LENGTH, KEY_VALUE_HEADS * HEAD_SIZE).astype(jnp.bfloat16)


def block_scale(stream_key, extent, cuts, least, high):
    level, own = 1.0, jax.random.fold_in(stream_key, 6)
    for axis_at, blocks in cuts:
        heights = jnp.exp(jax.random.uniform(jax.random.fold_in(own, axis_at), (blocks,), jnp.float32, least / len(cuts), high / len(cuts)))
        level = level * jnp.repeat(heights, extent[axis_at] // blocks).reshape([-1 if axis == axis_at else 1 for axis in range(len(extent))])
    return level


def noise(key, shape, width, reach, pieces=(), held_as=jnp.bfloat16):
    gain = block_scale(key, shape, pieces, -0.22, 0.18) if pieces else 1.0
    drawn = jax.random.normal(key, shape, jnp.float32) * width * gain
    return jnp.minimum(jnp.maximum(drawn, -reach), reach).astype(held_as)


def setup_inputs(seed: int = 0) -> dict:
    key_list = jax.random.split(jax.random.key(seed), 9)
    queries = draw_queries(jax.random.fold_in(key_list[8], 71), 0)
    rotated_key_rows = draw_rotated_key_rows(jax.random.fold_in(key_list[8], 71), 0)
    hidden_states = noise(key_list[2], (SEQUENCE_COUNT, SEQUENCE_LENGTH, D), 1.0, 6.0, ((0, 8), (1, 32)))
    block_order = jax.random.permutation(key_list[3], BLOCKS).astype(jnp.int32)
    first_weight = noise(key_list[4], (D, RETAIN_HIDDEN), D ** -0.5, 0.0625)
    first_bias = noise(key_list[5], (RETAIN_HIDDEN,), 0.5, 3.0, (), jnp.float32)
    output_weight = noise(key_list[6], (KEY_VALUE_HEADS, RETAIN_HIDDEN), RETAIN_HIDDEN ** -0.5, 0.25)
    output_bias = jnp.clip(jax.random.uniform(key_list[7], (KEY_VALUE_HEADS,), jnp.float32, -1.0, 1.0), -1.0, 1.0)
    return {"queries": queries, "rotated_key_rows": rotated_key_rows, "hidden_states": hidden_states, "block_order": block_order, "first_weight": first_weight, "first_bias": first_bias, "output_weight": output_weight, "output_bias": output_bias}


def places(block_order):
    row_ids = jnp.arange(SEQUENCE_LENGTH, dtype=jnp.int32)
    return block_order[row_ids // BLK].astype(jnp.int32) * BLK + row_ids % BLK

def sequence_mass(queries, rotated_key_rows, places_all):
    head_queries = queries.astype(jnp.float32).reshape(SEQUENCE_LENGTH, KEY_VALUE_HEADS, QUERY_GROUP_SIZE, HEAD_SIZE)
    head_keys = rotated_key_rows.astype(jnp.float32).reshape(SEQUENCE_LENGTH, KEY_VALUE_HEADS, HEAD_SIZE)
    height = math.gcd(SEQUENCE_LENGTH, 128)

    def visit_block(carried, step_index):
        query_block = lax.dynamic_slice_in_dim(head_queries, step_index * height, height, 0)
        query_pos = lax.dynamic_slice_in_dim(places_all, step_index * height, height, 0)
        scores = jnp.einsum('tkgd,nkd->kgtn', query_block, head_keys, precision=lax.Precision.HIGHEST) * HEAD_SIZE ** (-0.5)
        visible = query_pos[:, None] >= places_all[None, :]
        masked = jnp.where(visible, scores, -1e+30)
        highest = lax.optimization_barrier(jnp.max(masked, axis=-1))
        summed = lax.optimization_barrier(jnp.sum(jnp.where(visible, jnp.exp(masked - highest[..., None]), 0.0), axis=-1))
        log_total = highest + jnp.log(summed)
        weights = jnp.where(visible, jnp.exp(masked - log_total[..., None]), 0.0)
        return (carried + lax.optimization_barrier(jnp.sum(weights, axis=(1, 2))) / QUERY_GROUP_SIZE, None)
    every_step = jnp.arange(SEQUENCE_LENGTH // height, dtype=jnp.int32)
    key_attention_mass, ignored_value = lax.scan(visit_block, jnp.zeros((KEY_VALUE_HEADS, SEQUENCE_LENGTH), jnp.float32), every_step)
    return key_attention_mass

def normalized_scores(value_rows):
    return value_rows / jnp.sqrt(jnp.mean(value_rows * value_rows) + 1e-06)

def reference(queries, rotated_key_rows, hidden_states, block_order, first_weight, first_bias, output_weight, output_bias):
    places_all = places(block_order)
    token_attention_mass = lax.map(lambda paired: sequence_mass(paired[0], paired[1], places_all), (queries, rotated_key_rows))
    tokens_in = hidden_states.reshape(SEQUENCE_COUNT * SEQUENCE_LENGTH, D)
    pre_act = jnp.dot(tokens_in, first_weight, preferred_element_type=jnp.float32) + first_bias
    hidden = jax.nn.silu(pre_act).astype(jnp.bfloat16)
    predicted_scores = lax.dot_general(output_weight, hidden, (((1,), (1,)), ((), ())), preferred_element_type=jnp.float32) + output_bias[:, None]
    target_rows = jnp.transpose(token_attention_mass, (1, 0, 2)).reshape(KEY_VALUE_HEADS, SEQUENCE_COUNT * SEQUENCE_LENGTH)
    score_residue = predicted_scores - jnp.log(1.0 + target_rows)
    loss_value = 0.5 * jnp.sum(score_residue * score_residue) / SEQUENCE_LENGTH
    out_grad = score_residue / SEQUENCE_LENGTH
    grad_bias = lax.optimization_barrier(jnp.sum(out_grad, axis=1))
    grad_second = jnp.dot(out_grad, hidden.astype(jnp.float32), precision=lax.Precision.HIGHEST)
    back_grad = jnp.dot(out_grad.T, output_weight.astype(jnp.float32), precision=lax.Precision.HIGHEST)
    gate_value = jax.nn.sigmoid(pre_act)
    slope_grad = back_grad * gate_value * (1.0 + pre_act * (1.0 - gate_value))
    grad_first_bias = lax.optimization_barrier(jnp.sum(slope_grad, axis=0))
    slope_half = slope_grad.astype(jnp.bfloat16)
    grad_first = lax.dot_general(tokens_in, slope_half, (((0,), (0,)), ((), ())), preferred_element_type=jnp.float32)
    return (token_attention_mass, loss_value, normalized_scores(grad_first), normalized_scores(grad_second), normalized_scores(grad_first_bias), grad_bias)
```

```python
import functools
import math

import jax
import jax.numpy as jnp
from jax import lax
from jax.experimental import pallas as pl
from jax.experimental.pallas import tpu as pltpu
from jax.sharding import PartitionSpec as P

MESH = pl.DeviceIdType.MESH
ROWS = 128
BLK = 64
HEAD_SIZE = 128
KEY_VALUE_HEADS = 4
QUERY_GROUP_SIZE = 8
HIDDEN = 512
KEYS = 512
SCALE2 = HEAD_SIZE**-0.5 * math.log2(math.e)
LAST = (((1,), (1,)), ((), ()))
SEQ_PARTS = (4, 4, 2)


def dot_t(a, b, precision=None):
    return lax.dot_general(a, b, LAST, preferred_element_type=jnp.float32, precision=precision)


def attend(head, order_ref, me, slot_seq, q_buf, k_buf, p_buf, m_buf, mass_out, middle):
    steps = k_buf.shape[1] // KEYS
    width = QUERY_GROUP_SIZE * ROWS
    lane = lax.broadcasted_iota(jnp.int32, (BLK, ROWS), 1)
    low, high = order_ref[2 * me], order_ref[2 * me + 1]
    q_pos = jnp.where(lane < BLK, low, high) * BLK + lax.rem(lane, BLK)
    inner = lax.broadcasted_iota(jnp.int32, (BLK, ROWS), 0)

    def visit(step, carried):
        highest, summed = carried
        first = pl.multiple_of(step * KEYS, KEYS)
        keys = k_buf[head, pl.ds(first, KEYS), :]
        pieces = []
        for part in range(KEYS // BLK):
            owner = slot_seq(step * (KEYS // ROWS) + part // 2)
            k_pos = order_ref[2 * owner + part % 2] * BLK + inner
            pieces.append(jnp.where(k_pos <= q_pos, 0.0, -1e30))
        bias = jnp.concatenate(pieces, axis=0)
        bias = jnp.concatenate([bias, bias], axis=1)
        new_highest, new_summed = [], []
        for pair in range(QUERY_GROUP_SIZE // 2):
            start = pl.multiple_of((head * QUERY_GROUP_SIZE + 2 * pair) * ROWS, 2 * ROWS)
            score = dot_t(keys, q_buf[pl.ds(start, 2 * ROWS), :]) + bias
            old = highest[:, pair * 256 : pair * 256 + 256]
            top = jnp.maximum(old, jnp.max(score, axis=0, keepdims=True))
            weight = jnp.exp2((score - top) * SCALE2)
            total = summed[:, pair * 256 : pair * 256 + 256] * jnp.exp2((old - top) * SCALE2)
            new_highest.append(top)
            new_summed.append(total + jnp.sum(weight, axis=0, keepdims=True))
            p_buf[pl.ds(first, KEYS), pair * 256 : pair * 256 + 256] = weight.astype(jnp.bfloat16)
        highest = jnp.concatenate(new_highest, axis=1)
        m_buf[step, 0:1, :] = highest
        return highest, jnp.concatenate(new_summed, axis=1)

    start_state = (jnp.full((1, width), -1e30, jnp.float32), jnp.zeros((1, width), jnp.float32))
    highest, summed = lax.fori_loop(0, steps, visit, start_state)
    middle()
    inverse = 1.0 / (summed * QUERY_GROUP_SIZE)
    row = lax.broadcasted_iota(jnp.int32, (16, width), 0)

    def collect(step, _):
        first = pl.multiple_of(step * KEYS, KEYS)
        scale = jnp.exp2((m_buf[step, 0:1, :] - highest) * SCALE2) * inverse
        coarse = scale.astype(jnp.bfloat16).astype(jnp.float32)
        both = jnp.where(row == 0, coarse, jnp.where(row == 1, scale - coarse, 0.0))
        mass = dot_t(both.astype(jnp.bfloat16), p_buf[pl.ds(first, KEYS), :])
        line = mass[0:1, :] + mass[1:2, :]
        for part in range(KEYS // ROWS):
            mass_out[step * (KEYS // ROWS) + part, pl.ds(head, 1), :] = line[
                :, part * ROWS : part * ROWS + ROWS
            ]
        return _

    lax.fori_loop(0, steps, collect, 0)


class Gather:
    def __init__(self, view, where, sems):
        self.view, self.where, self.sems = view, where, sems

    def copy(self, block, stage, chunk, hop, device):
        send, recv = self.sems[2 * stage], self.sems[2 * stage + 1]
        place = (chunk, hop)
        return pltpu.make_async_remote_copy(
            src_ref=block,
            dst_ref=block,
            send_sem=send.at[place],
            recv_sem=recv.at[place],
            device_id=device,
            device_id_type=MESH,
        )

    def along_z(self, chunk):
        w = self.where
        return [
            self.copy(
                self.view(chunk, w.slot(w.y, w.z, w.c), 1), 0, chunk, hop,
                w.device(w.y, lax.rem(w.z + hop, w.nz), w.c),
            )
            for hop in range(1, w.nz)
        ]

    def along_y(self, chunk):
        w = self.where
        return [
            self.copy(
                self.view(chunk, w.slot(w.y, 0, w.c), w.nz), 1, chunk, hop,
                w.device(lax.rem(w.y + hop, w.ny), w.z, w.c),
            )
            for hop in range(1, w.ny)
        ]

    def across(self, chunk):
        w = self.where
        return [
            self.copy(
                self.view(chunk, w.slot(0, 0, w.c), w.ny * w.nz), 2, chunk, 0,
                w.device(w.y, w.z, 1 - w.c),
            )
        ]

    def first(self, chunk):
        for copy in self.along_z(chunk):
            copy.start()

    def second(self, chunk):
        w = self.where
        for hop in range(1, w.nz):
            block = self.view(chunk, w.slot(w.y, lax.rem(w.z + w.nz - hop, w.nz), w.c), 1)
            self.copy(block, 0, chunk, hop, w.device(w.y, w.z, 1 - w.c)).wait_recv()
        for copy in self.along_y(chunk):
            copy.start()

    def third(self, chunk):
        w = self.where
        for hop in range(1, w.ny):
            block = self.view(chunk, w.slot(lax.rem(w.y + w.ny - hop, w.ny), 0, w.c), w.nz)
            self.copy(block, 1, chunk, hop, w.device(w.y, w.z, 1 - w.c)).wait_recv()
        for copy in self.across(chunk):
            copy.start()

    def arrive(self, chunk):
        w = self.where
        block = self.view(chunk, w.slot(0, 0, 1 - w.c), w.ny * w.nz)
        self.copy(block, 2, chunk, 0, w.device(w.y, w.z, 1 - w.c)).wait_recv()

    def drain(self, chunk):
        for copy in self.along_z(chunk) + self.along_y(chunk) + self.across(chunk):
            copy.wait_send()


class Where:
    def __init__(self, parts):
        self.ny, self.nz, self.nc = parts
        self.dp, self.seq = lax.axis_index("dp"), lax.axis_index("seq")
        self.c = lax.rem(self.seq, self.nc)
        self.z = lax.rem(self.seq // self.nc, self.nz)
        self.y = self.seq // (self.nc * self.nz)

    def slot(self, y, z, c):
        return (c * self.ny + y) * self.nz + z

    def device(self, y, z, c):
        return (self.dp, (y * self.nz + z) * self.nc + c)

    def slot_seq(self, slot):
        plane = self.ny * self.nz
        return lax.rem(slot, plane) * self.nc + slot // plane

    def seq_slot(self, seq):
        return lax.rem(seq, self.nc) * (self.ny * self.nz) + seq // self.nc


def remote(src, dst, send, recv, device):
    return pltpu.make_async_remote_copy(
        src_ref=src, dst_ref=dst, send_sem=send, recv_sem=recv, device_id=device,
        device_id_type=MESH,
    )


def kernel(
    parts, ndp,
    order_ref, b2_ref, q_hbm, k_hbm, hs_hbm, w1_hbm, b1_ref, w2_ref,
    mass_ref, step_ref, second_ref, first_bias_ref, misc_ref,
    q_buf, k_buf, hs_buf, w1_buf, p_buf, m_buf, cols, s_buf, pre_buf, gate_buf, hid_buf,
    mass_out, mass_in, small_z, small_y, small_c, small_d,
    part_buf, piece_buf, full_buf, sq_seq, sq_dp,
    q_sem, k_sem, hs_sem, w1_sem, own_sem,
    kg0, kg1, kg2, kg3, kg4, kg5, sg0, sg1, sg2, sg3, sg4, sg5,
    a_send, a_recv, m_send, m_recv, z_send, z_recv, y_send, y_recv, c_send, c_recv,
    d_send, d_recv, p_send, p_recv, f_send, f_recv, e_send, e_recv, g_send, g_recv,
):
    w = Where(parts)
    ns = w.ny * w.nz * w.nc
    me, dp = w.seq, w.dp
    mine = w.slot(w.y, w.z, w.c)
    length = float(ns * ROWS)
    depth = hs_hbm.shape[1]
    wide = depth // ns
    height = HIDDEN // ndp
    heads = KEY_VALUE_HEADS

    def key_view(chunk, slot, amount):
        return k_buf.at[chunk, pl.ds(pl.multiple_of(slot * ROWS, ROWS), amount * ROWS), :]

    def slope_view(chunk, slot, amount):
        return s_buf.at[pl.ds(slot, amount), pl.ds(chunk * 128, 128), :]

    key_gather = Gather(key_view, w, (kg0, kg1, kg2, kg3, kg4, kg5))
    slope_gather = Gather(slope_view, w, (sg0, sg1, sg2, sg3, sg4, sg5))

    k_copies = [
        pltpu.make_async_copy(
            k_hbm.at[:, pl.ds(head * HEAD_SIZE, HEAD_SIZE)], key_view(head, mine, 1), k_sem.at[head]
        )
        for head in range(heads)
    ]
    for copy in k_copies:
        copy.start()
    quarters = 4
    span = depth // quarters

    def w1_copy(quarter):
        return pltpu.make_async_copy(
            w1_hbm.at[pl.ds(quarter * span, span), :], w1_buf.at[pl.ds(quarter * span, span), :],
            w1_sem.at[quarter],
        )

    hs_copy = pltpu.make_async_copy(hs_hbm, hs_buf, hs_sem.at[0])
    own_copy = pltpu.make_async_copy(
        hs_hbm.at[:, pl.ds(pl.multiple_of(me * wide, 128), wide)], cols.at[mine], own_sem.at[0]
    )

    def q_copy(head):
        return pltpu.make_async_copy(
            q_hbm.at[:, pl.ds(pl.multiple_of(head * HEAD_SIZE, 128), HEAD_SIZE)],
            q_buf.at[pl.ds(pl.multiple_of(head * ROWS, ROWS), ROWS), :],
            q_sem.at[head],
        )

    hs_copy.start()
    for quarter in range(quarters):
        w1_copy(quarter).start()
    own_copy.start()

    barrier = pltpu.get_barrier_semaphore()

    def greet_seq(hop, _):
        pl.semaphore_signal(
            barrier, inc=1, device_id=(dp, lax.rem(me + hop, ns)), device_id_type=MESH
        )
        return _

    def greet_dp(hop, _):
        pl.semaphore_signal(
            barrier, inc=1, device_id=(lax.rem(dp + hop, ndp), me), device_id_type=MESH
        )
        return _

    lax.fori_loop(1, ns, greet_seq, 0)
    lax.fori_loop(1, ndp, greet_dp, 0)

    def q_start(head, _):
        q_copy(head).start()
        return _

    lax.fori_loop(0, heads * QUERY_GROUP_SIZE, q_start, 0)
    for copy in k_copies:
        copy.wait()
    pl.semaphore_wait(barrier, ns - 1 + ndp - 1)
    for head in range(heads):
        key_gather.first(head)

    hs_copy.wait()
    pre_buf[...] = jnp.broadcast_to(b1_ref[...], (ROWS, HIDDEN))
    for quarter in range(quarters):
        w1_copy(quarter).wait()

        def project(tile, _):
            at = pl.multiple_of(quarter * span + tile * 256, 256)
            pre_buf[...] += jnp.dot(
                hs_buf[:, pl.ds(at, 256)], w1_buf[pl.ds(at, 256), :],
                preferred_element_type=jnp.float32,
            )
            return _

        lax.fori_loop(0, span // 256, project, 0)
        key_gather.second(quarter)

    def a_copy(hop):
        to = lax.rem(me + hop, ns)
        return remote(
            hs_hbm.at[:, pl.ds(pl.multiple_of(to * wide, 128), wide)], cols.at[mine],
            a_send.at[hop], a_recv.at[hop], (dp, to),
        )

    def a_start(hop, _):
        a_copy(hop).start()
        return _

    lax.fori_loop(1, ns, a_start, 0)
    key_gather.third(0)

    pre = jnp.transpose(pre_buf[...])
    gate = 1.0 / (1.0 + jnp.exp(-pre))
    gate_buf[...] = gate * (1.0 + pre * (1.0 - gate))
    hid_buf[...] = (pre * gate).astype(jnp.bfloat16)

    def q_wait(head, _):
        q_copy(head).wait()
        return _

    lax.fori_loop(0, heads * QUERY_GROUP_SIZE, q_wait, 0)

    def one_head(head, _):
        key_gather.arrive(head)

        def middle():
            @pl.when(head < heads - 1)
            def _():
                key_gather.third(head + 1)

        attend(head, order_ref, me, w.slot_seq, q_buf, k_buf, p_buf, m_buf, mass_out, middle)
        return _

    lax.fori_loop(0, heads, one_head, 0)

    def m_copy(hop):
        to = lax.rem(me + hop, ns)
        return remote(
            mass_out.at[w.seq_slot(to)], mass_in.at[hop], m_send.at[hop], m_recv.at[hop], (dp, to)
        )

    def m_start(hop, _):
        m_copy(hop).start()
        return _

    lax.fori_loop(1, ns, m_start, 0)
    predicted = jnp.dot(w2_ref[...], hid_buf[...], preferred_element_type=jnp.float32)
    line = lax.broadcasted_iota(jnp.int32, (heads, ROWS), 0)
    for head in range(heads):
        predicted += jnp.where(line == head, b2_ref[head], 0.0)

    def m_add(hop, total):
        m_copy(hop).wait_recv()
        return total + mass_in[hop]

    mass = lax.fori_loop(1, ns, m_add, mass_out[mine])[0:heads, :]
    mass_ref[...] = mass
    residue = predicted - jnp.log(1.0 + mass)
    out_grad = residue / length
    w2_wide = jnp.concatenate(
        [w2_ref[...].astype(jnp.float32), jnp.zeros((8 - heads, HIDDEN), jnp.float32)], axis=0
    )
    w2_turned = jnp.transpose(w2_wide)
    back = w2_turned[:, 0:1] * out_grad[0:1, :]
    for head in range(1, heads):
        back += w2_turned[:, head : head + 1] * out_grad[head : head + 1, :]
    slope = back * gate_buf[...]
    s_buf[mine] = slope.astype(jnp.bfloat16)
    for chunk in range(4):
        slope_gather.first(chunk)

    def exchange(buf, at, count, send, recv, device):
        return [
            remote(buf.at[at], buf.at[at], send.at[hop], recv.at[hop], device(hop))
            for hop in range(1, count)
        ]

    def z_copies():
        return exchange(
            small_z, w.z, w.nz, z_send, z_recv,
            lambda hop: w.device(w.y, lax.rem(w.z + hop, w.nz), w.c),
        )

    def y_copies():
        return exchange(
            small_y, w.y, w.ny, y_send, y_recv,
            lambda hop: w.device(lax.rem(w.y + hop, w.ny), w.z, w.c),
        )

    def c_copies():
        return exchange(
            small_c, w.c, w.nc, c_send, c_recv, lambda hop: w.device(w.y, w.z, 1 - w.c)
        )

    def d_copies():
        return exchange(
            small_d, dp, ndp, d_send, d_recv, lambda hop: (lax.rem(dp + hop, ndp), me)
        )

    def settle(copies, buf):
        for copy in copies:
            copy.wait_recv()
        total = buf[0]
        for at in range(1, buf.shape[0]):
            total += buf[at]
        return total

    exact = lax.Precision.HIGHEST
    second = dot_t(out_grad, hid_buf[...].astype(jnp.float32), exact)
    ones = jnp.ones((8, ROWS), jnp.float32)
    first_bias = dot_t(ones, slope, exact)[0:1, :]
    place = lax.broadcasted_iota(jnp.int32, (1, HIDDEN), 1)
    bias_sum = jnp.sum(out_grad, axis=1, keepdims=True)
    loss = 0.5 * jnp.sum(jnp.sum(residue * residue, axis=1, keepdims=True), axis=0, keepdims=True)
    last = jnp.where(place == heads, loss / length, 0.0)
    for head in range(heads):
        last = jnp.where(place == head, bias_sum[head : head + 1, :], last)
    small = jnp.concatenate(
        [second, first_bias, last, jnp.zeros((2, HIDDEN), jnp.float32)], axis=0
    )
    small_z[w.z] = small
    for copy in z_copies():
        copy.start()

    for chunk in range(4):
        slope_gather.second(chunk)
    small_y[w.y] = settle(z_copies(), small_z)
    for copy in y_copies():
        copy.start()
    for chunk in range(4):
        slope_gather.third(chunk)
    small_c[w.c] = settle(y_copies(), small_y)
    for copy in c_copies():
        copy.start()

    own_copy.wait()

    def a_wait(hop, _):
        a_copy(hop).wait_recv()
        return _

    lax.fori_loop(1, ns, a_wait, 0)
    small_d[dp] = settle(c_copies(), small_c)
    for copy in d_copies():
        copy.start()

    def p_copy(hop):
        to = lax.rem(dp + hop, ndp)
        return remote(
            part_buf.at[pl.ds(pl.multiple_of(to * height, height), height), :], piece_buf.at[dp],
            p_send.at[hop], p_recv.at[hop], (to, me),
        )

    half = HIDDEN // 2
    for side in range(2):
        rows = pl.ds(side * half, half)
        slope_gather.arrive(2 * side)
        slope_gather.arrive(2 * side + 1)

        def gather_grad(at, total):
            return total + jnp.dot(
                s_buf[at, rows, :], cols[at], preferred_element_type=jnp.float32
            )

        part_buf[rows, :] = lax.fori_loop(
            0, ns, gather_grad, jnp.zeros((half, wide), jnp.float32)
        )
    for hop in range(1, ndp):
        p_copy(hop).start()
    piece_buf[dp] = part_buf[pl.ds(pl.multiple_of(dp * height, height), height), :]
    for hop in range(1, ndp):
        p_copy(hop).wait_recv()
    piece = piece_buf[0]
    for at in range(1, ndp):
        piece += piece_buf[at]
    own_rows = pl.ds(pl.multiple_of(dp * height, height), height)
    full_buf[own_rows, :] = piece

    def f_copy(hop):
        to = lax.rem(dp + hop, ndp)
        return remote(
            full_buf.at[own_rows, :], full_buf.at[own_rows, :], f_send.at[hop], f_recv.at[hop],
            (to, me),
        )

    for hop in range(1, ndp):
        f_copy(hop).start()
    squares = piece * piece
    squares = squares[:, 0:128] + squares[:, 128:256]
    sq_seq[me] = jnp.sum(squares.reshape(height // 8, 8, 128), axis=0)

    def e_copy(hop):
        return remote(
            sq_seq.at[me], sq_seq.at[me], e_send.at[hop], e_recv.at[hop],
            (dp, lax.rem(me + hop, ns)),
        )

    def e_start(hop, _):
        e_copy(hop).start()
        return _

    def e_wait(hop, _):
        e_copy(hop).wait_recv()
        return _

    lax.fori_loop(1, ns, e_start, 0)

    small = settle(d_copies(), small_d)
    second = small[0:heads, :]

    def inverse_root(square_sum, entries):
        return 1.0 / jnp.sqrt(square_sum / entries + 1e-06)

    def whole_sum(x):
        return jnp.sum(jnp.sum(x, axis=1, keepdims=True), axis=0, keepdims=True)

    second_ref[...] = second * inverse_root(whole_sum(second * second), heads * HIDDEN)
    first_bias = small[4:5, :]
    first_bias_ref[...] = first_bias * inverse_root(whole_sum(first_bias * first_bias), HIDDEN)
    misc_ref[...] = small[5:6, 0:128]

    lax.fori_loop(1, ns, e_wait, 0)
    square = sq_seq[0]
    for at in range(1, ns):
        square += sq_seq[at]
    sq_dp[dp] = square

    def g_copy(hop):
        return remote(
            sq_dp.at[dp], sq_dp.at[dp], g_send.at[hop], g_recv.at[hop],
            (lax.rem(dp + hop, ndp), me),
        )

    for hop in range(1, ndp):
        g_copy(hop).start()
    for hop in range(1, ndp):
        f_copy(hop).wait_recv()
    turned = jnp.transpose(full_buf[...])
    for hop in range(1, ndp):
        g_copy(hop).wait_recv()
    square = sq_dp[0]
    for at in range(1, ndp):
        square += sq_dp[at]
    step_ref[...] = turned * inverse_root(whole_sum(square), depth * HIDDEN)

    def drain(hop, _):
        a_copy(hop).wait_send()
        m_copy(hop).wait_send()
        e_copy(hop).wait_send()
        return _

    lax.fori_loop(1, ns, drain, 0)
    for chunk in range(4):
        key_gather.drain(chunk)
        slope_gather.drain(chunk)
    for copy in z_copies() + y_copies() + c_copies() + d_copies():
        copy.wait_send()
    for hop in range(1, ndp):
        p_copy(hop).wait_send()
        f_copy(hop).wait_send()
        g_copy(hop).wait_send()


def per_device(parts, ndp, ns, queries, key_rows, hidden, order, w1, b1, w2, b2):
    f32, bf16 = jnp.float32, jnp.bfloat16
    depth = hidden.shape[2]
    wide = depth // ns
    height = HIDDEN // ndp
    vmem, smem, anywhere = (
        pl.BlockSpec(memory_space=pltpu.VMEM),
        pl.BlockSpec(memory_space=pltpu.SMEM),
        pl.BlockSpec(memory_space=pl.ANY),
    )
    ny, nz, nc = parts
    dma = pltpu.SemaphoreType.DMA
    gather_sems = [dma((4, n)) for n in (nz, nz, ny, ny, 1, 1)]
    heads = KEY_VALUE_HEADS
    mass, step, second, first_bias, misc = pl.pallas_call(
        functools.partial(kernel, parts, ndp),
        out_shape=(
            jax.ShapeDtypeStruct((heads, ROWS), f32),
            jax.ShapeDtypeStruct((wide, HIDDEN), f32),
            jax.ShapeDtypeStruct((heads, HIDDEN), f32),
            jax.ShapeDtypeStruct((1, HIDDEN), f32),
            jax.ShapeDtypeStruct((1, 128), f32),
        ),
        in_specs=[smem, smem, anywhere, anywhere, anywhere, anywhere, vmem, vmem],
        out_specs=(vmem,) * 5,
        scratch_shapes=[
            pltpu.VMEM((heads * QUERY_GROUP_SIZE * ROWS, HEAD_SIZE), bf16),
            pltpu.VMEM((heads, ns * ROWS, HEAD_SIZE), bf16),
            pltpu.VMEM((ROWS, depth), bf16),
            pltpu.VMEM((depth, HIDDEN), bf16),
            pltpu.VMEM((ns * ROWS, QUERY_GROUP_SIZE * ROWS), bf16),
            pltpu.VMEM((ns * ROWS // KEYS, 8, QUERY_GROUP_SIZE * ROWS), f32),
            pltpu.VMEM((ns, ROWS, wide), bf16),
            pltpu.VMEM((ns, HIDDEN, ROWS), bf16),
            pltpu.VMEM((ROWS, HIDDEN), f32),
            pltpu.VMEM((HIDDEN, ROWS), f32),
            pltpu.VMEM((HIDDEN, ROWS), bf16),
            pltpu.VMEM((ns, 8, ROWS), f32),
            pltpu.VMEM((ns, 8, ROWS), f32),
            pltpu.VMEM((nz, 8, HIDDEN), f32),
            pltpu.VMEM((ny, 8, HIDDEN), f32),
            pltpu.VMEM((nc, 8, HIDDEN), f32),
            pltpu.VMEM((ndp, 8, HIDDEN), f32),
            pltpu.VMEM((HIDDEN, wide), f32),
            pltpu.VMEM((ndp, height, wide), f32),
            pltpu.VMEM((HIDDEN, wide), f32),
            pltpu.VMEM((ns, 8, 128), f32),
            pltpu.VMEM((ndp, 8, 128), f32),
            dma((heads * QUERY_GROUP_SIZE,)), dma((4,)), dma((1,)), dma((4,)), dma((1,)),
            *gather_sems, *gather_sems,
            dma((ns,)), dma((ns,)), dma((ns,)), dma((ns,)),
            dma((nz,)), dma((nz,)), dma((ny,)), dma((ny,)), dma((nc,)), dma((nc,)),
            dma((ndp,)), dma((ndp,)), dma((ndp,)), dma((ndp,)), dma((ndp,)), dma((ndp,)),
            dma((ns,)), dma((ns,)), dma((ndp,)), dma((ndp,)),
        ],
        compiler_params=pltpu.CompilerParams(
            collective_id=0, has_side_effects=True, vmem_limit_bytes=60 * 1024 * 1024
        ),
    )(
        order, b2, queries.reshape(ROWS, -1), key_rows.reshape(ROWS, -1),
        hidden.reshape(ROWS, depth), w1, b1.reshape(1, HIDDEN), w2,
    )
    return (
        mass.reshape(1, heads, ROWS), misc[0, heads], step, second, first_bias.reshape(HIDDEN),
        misc[0, 0:heads],
    )


def solution(mesh, parts=SEQ_PARTS):
    in_specs = (P("dp", "seq", None),) * 3 + (P(),) * 5
    out_specs = (P("dp", None, "seq"), P(), P("seq", None), P(), P(), P())
    body = functools.partial(per_device, parts, mesh.shape["dp"], mesh.shape["seq"])
    return jax.shard_map(
        body, mesh=mesh, in_specs=in_specs, out_specs=out_specs, check_vma=False
    )
```

```python
import functools
import math

import jax
import jax.numpy as jnp
from jax import lax
from jax.experimental import pallas as pl
from jax.experimental.pallas import tpu as pltpu
from jax.sharding import PartitionSpec as P

MESH = pl.DeviceIdType.MESH
ROWS = 128
BLK = 64
HEAD_SIZE = 128
HEADS = 4
GROUP = 8
HIDDEN = 512
KEYS = 512
CHUNKS = 4
SCALE2 = HEAD_SIZE**-0.5 * math.log2(math.e)
LAST = (((1,), (1,)), ((), ()))
DP_PARTS = (2, 4)
SEQ_PARTS = (4, 4, 2)


def dot_t(a, b, precision=None):
    return lax.dot_general(a, b, LAST, preferred_element_type=jnp.float32, precision=precision)


def dot(a, b, precision=None):
    return jnp.dot(a, b, preferred_element_type=jnp.float32, precision=precision)


def ring(at, hop, size):
    return lax.rem(at + hop, size)


def remote(src, dst, send, recv, device):
    return pltpu.make_async_remote_copy(
        src_ref=src, dst_ref=dst, send_sem=send, recv_sem=recv, device_id=device,
        device_id_type=MESH,
    )


class Where:
    def __init__(self, dp_parts, seq_parts):
        self.nl, self.nx = dp_parts
        self.ny, self.nz, self.nc = seq_parts
        self.dp, self.seq = lax.axis_index("dp"), lax.axis_index("seq")
        self.x, self.l = lax.rem(self.dp, self.nx), self.dp // self.nx
        self.c = lax.rem(self.seq, self.nc)
        self.z = lax.rem(self.seq // self.nc, self.nz)
        self.y = self.seq // (self.nc * self.nz)

    def device(self, x=None, y=None, z=None, l=None, c=None):
        x, y, z, l, c = (
            own if given is None else given
            for given, own in zip((x, y, z, l, c), (self.x, self.y, self.z, self.l, self.c))
        )
        return (l * self.nx + x, (y * self.nz + z) * self.nc + c)


class Gather:
    def __init__(self, w, axis, view, y_first, sems):
        self.w, self.axis, self.view, self.sems, self.y_first = w, axis, view, sems, y_first
        self.b, self.nb = (w.z, w.nz) if axis == "z" else (w.x, w.nx)

    def copy(self, block, stage, chunk, hop, device):
        place = (chunk, hop)
        return remote(
            block, block, self.sems[2 * stage].at[place], self.sems[2 * stage + 1].at[place], device
        )

    def sent(self, chunk, stage):
        w = self.w
        y_step = stage == (0 if chunk in self.y_first else 1)
        if stage == 2:
            return [(self.view(chunk, w.c), 0, w.device(c=1 - w.c))]
        if stage == 0:
            block = self.view(chunk, w.c, w.y, self.b)
        elif y_step:
            block = self.view(chunk, w.c, w.y)
        else:
            block = self.view(chunk, w.c, slice(None), self.b)
        if y_step:
            return [(block, hop, w.device(y=ring(w.y, hop, w.ny))) for hop in range(1, w.ny)]
        return [
            (block, hop, w.device(**{self.axis: ring(self.b, hop, self.nb)}))
            for hop in range(1, self.nb)
        ]

    def received(self, chunk, stage):
        w = self.w
        y_step = stage == (0 if chunk in self.y_first else 1)
        if stage == 2:
            return [(self.view(chunk, 1 - w.c), 0)]
        result = []
        for hop in range(1, w.ny if y_step else self.nb):
            if y_step:
                at_y, at_b = ring(w.y, w.ny - hop, w.ny), self.b
            else:
                at_y, at_b = w.y, ring(self.b, self.nb - hop, self.nb)
            if stage == 0:
                block = self.view(chunk, w.c, at_y, at_b)
            elif y_step:
                block = self.view(chunk, w.c, at_y)
            else:
                block = self.view(chunk, w.c, slice(None), at_b)
            result.append((block, hop))
        return result

    def start(self, chunk, stage):
        for block, hop, device in self.sent(chunk, stage):
            self.copy(block, stage, chunk, hop, device).start()

    def arrive(self, chunk, stage):
        for block, hop in self.received(chunk, stage):
            self.copy(block, stage, chunk, hop, self.w.device(c=1 - self.w.c)).wait_recv()

    def forward(self, chunk, stage):
        self.arrive(chunk, stage - 1)
        self.start(chunk, stage)

    def drain(self, chunk):
        for stage in range(3):
            for block, hop, device in self.sent(chunk, stage):
                self.copy(block, stage, chunk, hop, device).wait_send()


def attend(head, order_ref, w, q_buf, k_buf, p_buf, m_buf, mass_out, before, middle):
    steps = w.nc * w.ny
    keys_here = w.nz * ROWS
    width = GROUP * ROWS
    lane = lax.broadcasted_iota(jnp.int32, (BLK, ROWS), 1)
    low, high = order_ref[2 * w.seq], order_ref[2 * w.seq + 1]
    q_pos = jnp.where(lane < BLK, low, high) * BLK + lax.rem(lane, BLK)
    inner = lax.broadcasted_iota(jnp.int32, (BLK, ROWS), 0)

    def visit(step, carried):
        before(step)
        highest, summed = carried
        c, y = lax.rem(w.c + step // w.ny, w.nc), lax.rem(w.y + step, w.ny)
        keys = k_buf[head, c, y].reshape(keys_here, HEAD_SIZE)
        pieces = []
        for part in range(keys_here // BLK):
            owner = (y * w.nz + part // 2) * w.nc + c
            k_pos = order_ref[2 * owner + part % 2] * BLK + inner
            pieces.append(jnp.where(k_pos <= q_pos, 0.0, -1e30))
        bias = jnp.concatenate(pieces, axis=0)
        bias = jnp.concatenate([bias, bias], axis=1)
        new_highest, new_summed = [], []
        for pair in range(GROUP // 2):
            start = pl.multiple_of((head * GROUP + 2 * pair) * ROWS, 2 * ROWS)
            score = dot_t(keys, q_buf[pl.ds(start, 2 * ROWS), :]) + bias
            old = highest[:, pair * 256 : pair * 256 + 256]
            top = jnp.maximum(old, jnp.max(score, axis=0, keepdims=True))
            weight = jnp.exp2((score - top) * SCALE2)
            total = summed[:, pair * 256 : pair * 256 + 256] * jnp.exp2((old - top) * SCALE2)
            new_highest.append(top)
            new_summed.append(total + jnp.sum(weight, axis=0, keepdims=True))
            p_buf[step, :, pair * 256 : pair * 256 + 256] = weight.astype(jnp.bfloat16)
        highest = jnp.concatenate(new_highest, axis=1)
        m_buf[step, 0:1, :] = highest
        return highest, jnp.concatenate(new_summed, axis=1)

    start_state = (jnp.full((1, width), -1e30, jnp.float32), jnp.zeros((1, width), jnp.float32))
    highest, summed = lax.fori_loop(0, steps, visit, start_state)
    middle()
    inverse = 1.0 / (summed * GROUP)
    row = lax.broadcasted_iota(jnp.int32, (16, width), 0)

    def collect(step, _):
        scale = jnp.exp2((m_buf[step, 0:1, :] - highest) * SCALE2) * inverse
        coarse = scale.astype(jnp.bfloat16).astype(jnp.float32)
        both = jnp.where(row == 0, coarse, jnp.where(row == 1, scale - coarse, 0.0))
        mass = dot_t(both.astype(jnp.bfloat16), p_buf[step])
        line = mass[0:1, :] + mass[1:2, :]
        c, y = lax.rem(w.c + step // w.ny, w.nc), lax.rem(w.y + step, w.ny)
        for part in range(w.nz):
            mass_out[(y * w.nz + part) * w.nc + c, pl.ds(head, 1), :] = line[
                :, part * ROWS : part * ROWS + ROWS
            ]
        return _

    lax.fori_loop(0, steps, collect, 0)


def inverse_root(square_sum, entries):
    return 1.0 / jnp.sqrt(square_sum / entries + 1e-06)


def whole_sum(x):
    return jnp.sum(jnp.sum(x, axis=1, keepdims=True), axis=0, keepdims=True)


def kernel(
    dp_parts, seq_parts,
    order_ref, b2_ref, q_hbm, k_hbm, hs_hbm, w1_hbm, b1_ref, w2_ref,
    step_ref, small_ref,
    q_buf, k_buf, hs_buf, turned, w1_buf, p_buf, m_buf, cols, s_buf, pre_buf, gate_buf, hid_buf,
    mass_out, mass_in, small_z, small_y, small_c, small_d,
    part_buf, piece_buf, full_buf, sq_seq, sq_dp,
    q_sem, k_sem, hs_sem, w1_sem,
    kg0, kg1, kg2, kg3, kg4, kg5, sg0, sg1, sg2, sg3, sg4, sg5,
    a_send, a_recv, m_send, m_recv, z_send, z_recv, y_send, y_recv, c_send, c_recv,
    d_send, d_recv, p_send, p_recv, f_send, f_recv, e_send, e_recv, g_send, g_recv,
):
    w = Where(dp_parts, seq_parts)
    ns, ndp, plane = w.ny * w.nz * w.nc, w.nl * w.nx, w.nc * w.ny * w.nx
    me, dp = w.seq, w.dp
    length = float(ns * ROWS)
    depth = hs_hbm.shape[1]
    wide = depth // ns
    sub = wide // w.nx
    side_width = HIDDEN // w.nl

    def key_view(chunk, *at):
        return k_buf.at[(chunk, *at)]

    def slope_view(chunk, *at):
        at = at + (slice(None),) * (4 - len(at))
        return s_buf.at[(*at, pl.ds(chunk * 128, 128))]

    key_gather = Gather(w, "z", key_view, (), (kg0, kg1, kg2, kg3, kg4, kg5))
    slope_gather = Gather(w, "x", slope_view, (1, 3), (sg0, sg1, sg2, sg3, sg4, sg5))

    k_copies = [
        pltpu.make_async_copy(
            k_hbm.at[:, pl.ds(head * HEAD_SIZE, HEAD_SIZE)], key_view(head, w.c, w.y, w.z),
            k_sem.at[head],
        )
        for head in range(HEADS)
    ]
    for copy in k_copies:
        copy.start()

    barrier = pltpu.get_barrier_semaphore()

    def greet(device):
        pl.semaphore_signal(barrier, inc=1, device_id=device, device_id_type=MESH)

    def greet_seq(hop, _):
        greet((dp, ring(me, hop, ns)))
        return _

    def in_plane(index):
        return lax.rem(index, w.nx), lax.rem(index // w.nx, w.ny), index // (w.nx * w.ny)

    own_plane = (w.c * w.ny + w.y) * w.nx + w.x

    def plane_device(hop):
        x, y, c = in_plane(ring(own_plane, hop, plane))
        return w.device(x=x, y=y, c=c)

    def greet_plane(hop, _):
        greet(plane_device(hop))
        return _

    def greet_dp(hop, _):
        greet((ring(dp, hop, ndp), me))
        return _

    own_column = w.z * w.nl + w.l
    column = w.nz * w.nl

    def greet_column(hop, _):
        at = ring(own_column, hop, column)
        greet(w.device(z=at // w.nl, l=lax.rem(at, w.nl)))
        return _

    lax.fori_loop(1, ns, greet_seq, 0)
    lax.fori_loop(1, plane, greet_plane, 0)
    lax.fori_loop(1, ndp, greet_dp, 0)
    lax.fori_loop(1, column, greet_column, 0)

    quarters = CHUNKS
    span = depth // quarters

    def w1_copy(quarter):
        return pltpu.make_async_copy(
            w1_hbm.at[pl.ds(quarter * span, span), :], w1_buf.at[pl.ds(quarter * span, span), :],
            w1_sem.at[quarter],
        )

    hs_copy = pltpu.make_async_copy(hs_hbm, hs_buf, hs_sem.at[0])
    hs_copy.start()
    for quarter in range(quarters):
        w1_copy(quarter).start()

    def q_copy(head):
        return pltpu.make_async_copy(
            q_hbm.at[:, pl.ds(pl.multiple_of(head * HEAD_SIZE, 128), HEAD_SIZE)],
            q_buf.at[pl.ds(pl.multiple_of(head * ROWS, ROWS), ROWS), :],
            q_sem.at[head],
        )

    def q_start(head, _):
        q_copy(head).start()
        return _

    lax.fori_loop(0, HEADS * GROUP, q_start, 0)

    tiles = 128 // math.gcd(sub, 128)
    rows_of = min(sub, 128)

    def turn(tile, _):
        value = jnp.transpose(hs_buf[:, pl.ds(pl.multiple_of(tile * 128, 128), 128)])
        block, inside = tile // (wide // 128), lax.rem(tile, wide // 128)
        c = lax.rem(block, w.nc)
        z = lax.rem(block // w.nc, w.nz)
        y = block // (w.nc * w.nz)
        if sub <= 128:
            turned[y, z, c, pl.ds(inside * tiles, tiles)] = value.reshape(tiles, rows_of, ROWS)
        else:
            per = sub // 128
            start = pl.multiple_of(lax.rem(inside, per) * 128, 128)
            turned[y, z, c, inside // per, pl.ds(start, 128), :] = value
        return _

    for copy in k_copies:
        copy.wait()
    pl.semaphore_wait(barrier, ns - 1 + plane - 1 + ndp - 1 + column - 1)
    for head in range(HEADS):
        key_gather.start(head, 0)
    hs_copy.wait()

    pre_buf[...] = jnp.broadcast_to(b1_ref[...], (ROWS, HIDDEN))
    per_quarter = depth // 128 // quarters
    deep = min(1024, span)
    for quarter in range(quarters):
        w1_copy(quarter).wait()

        def project(tile, _):
            at = pl.multiple_of(quarter * span + tile * deep, deep)
            pre_buf[...] += dot(hs_buf[:, pl.ds(at, deep)], w1_buf[pl.ds(at, deep), :])
            return _

        lax.fori_loop(0, span // deep, project, 0)
        lax.fori_loop(quarter * per_quarter, (quarter + 1) * per_quarter, turn, 0)
        if quarter:
            key_gather.forward(quarter - 1, 1)
    key_gather.forward(CHUNKS - 1, 1)

    pre = pre_buf[...]
    gate = 1.0 / (1.0 + jnp.exp(-pre))
    gate_buf[...] = gate * (1.0 + pre * (1.0 - gate))
    hid_buf[...] = (pre * gate).astype(jnp.bfloat16)

    own_cols = cols.at[:, :, pl.ds(pl.multiple_of(own_plane * ROWS, ROWS), ROWS)]

    def a_copy(hop):
        x, y, c = in_plane(ring(own_plane, hop, plane))
        return remote(
            turned.at[y, :, c, x], own_cols, a_send.at[hop], a_recv.at[hop],
            w.device(x=x, y=y, c=c),
        )

    def a_start(hop, _):
        a_copy(hop).start()
        return _

    def q_wait(head, _):
        q_copy(head).wait()
        return _

    lax.fori_loop(0, HEADS * GROUP, q_wait, 0)
    cols[:, :, pl.ds(pl.multiple_of(own_plane * ROWS, ROWS), ROWS)] = turned[w.y, :, w.c, w.x]

    def one_head(head, _):
        def before(step):
            @pl.when((head == 0) & (step == 1))
            def _():
                key_gather.forward(0, 2)

            @pl.when(step == w.ny)
            def _():
                key_gather.arrive(head, 2)

        def middle():
            @pl.when(head < HEADS - 1)
            def _():
                key_gather.forward(head + 1, 2)

            @pl.when(head == 1)
            def _():
                lax.fori_loop(1, plane, a_start, 0)

        attend(head, order_ref, w, q_buf, k_buf, p_buf, m_buf, mass_out, before, middle)
        return _

    lax.fori_loop(0, HEADS, one_head, 0)

    def m_copy(hop):
        to = ring(me, hop, ns)
        return remote(mass_out.at[to], mass_in.at[hop], m_send.at[hop], m_recv.at[hop], (dp, to))

    def m_start(hop, _):
        m_copy(hop).start()
        return _

    lax.fori_loop(1, ns, m_start, 0)
    predicted = dot_t(w2_ref[...], hid_buf[...])
    line = lax.broadcasted_iota(jnp.int32, (HEADS, ROWS), 0)
    for head in range(HEADS):
        predicted += jnp.where(line == head, b2_ref[head], 0.0)

    for chunk in range(CHUNKS):
        key_gather.drain(chunk)

    def m_add(hop, total):
        m_copy(hop).wait_recv()
        return total + mass_in[hop]

    mass = lax.fori_loop(1, ns, m_add, mass_out[me])
    residue = predicted - jnp.log(1.0 + mass)
    out_grad = residue / length
    turned_grad = jnp.transpose(
        jnp.concatenate([out_grad, jnp.zeros((8 - HEADS, ROWS), jnp.float32)], axis=0)
    )
    w2_wide = w2_ref[...].astype(jnp.float32)
    back = turned_grad[:, 0:1] * w2_wide[0:1, :]
    for head in range(1, HEADS):
        back += turned_grad[:, head : head + 1] * w2_wide[head : head + 1, :]
    slope = back * gate_buf[...]
    s_buf[w.c, w.y, w.x] = slope.astype(jnp.bfloat16)
    for chunk in range(CHUNKS):
        slope_gather.start(chunk, 0)

    def exchange(buf, at, count, send, recv, device):
        return [
            remote(buf.at[at], buf.at[at], send.at[hop], recv.at[hop], device(hop))
            for hop in range(1, count)
        ]

    def z_copies():
        return exchange(
            small_z, w.z, w.nz, z_send, z_recv, lambda hop: w.device(z=ring(w.z, hop, w.nz))
        )

    def y_copies():
        return exchange(
            small_y, w.y, w.ny, y_send, y_recv, lambda hop: w.device(y=ring(w.y, hop, w.ny))
        )

    def c_copies():
        return exchange(small_c, w.c, w.nc, c_send, c_recv, lambda hop: w.device(c=1 - w.c))

    def d_copies():
        return exchange(small_d, dp, ndp, d_send, d_recv, lambda hop: (ring(dp, hop, ndp), me))

    def settle(copies, buf):
        for copy in copies:
            copy.wait_recv()
        total = buf[0]
        for at in range(1, buf.shape[0]):
            total += buf[at]
        return total

    exact = lax.Precision.HIGHEST
    second = dot(out_grad, hid_buf[...].astype(jnp.float32), exact)
    first_bias = jnp.sum(slope, axis=0, keepdims=True)
    place = lax.broadcasted_iota(jnp.int32, (1, HIDDEN), 1)
    bias_sum = jnp.sum(out_grad, axis=1, keepdims=True)
    loss = 0.5 * whole_sum(residue * residue)
    last = jnp.where(place == HEADS, loss / length, 0.0)
    for head in range(HEADS):
        last = jnp.where(place == head, bias_sum[head : head + 1, :], last)
    small_z[w.z] = jnp.concatenate(
        [second, first_bias, last, jnp.zeros((2, HIDDEN), jnp.float32)], axis=0
    )
    for copy in z_copies():
        copy.start()

    def m_drain(hop, _):
        m_copy(hop).wait_send()
        return _

    lax.fori_loop(1, ns, m_drain, 0)
    for chunk in range(CHUNKS):
        slope_gather.forward(chunk, 1)
    small_y[w.y] = settle(z_copies(), small_z)
    for copy in y_copies():
        copy.start()
    slope_gather.forward(0, 2)
    slope_gather.forward(1, 2)

    def a_wait(hop, _):
        a_copy(hop).wait()
        return _

    lax.fori_loop(1, plane, a_wait, 0)

    def p_copy(side, hop):
        to = ring(w.z, hop, w.nz)
        return remote(
            part_buf.at[side, to], piece_buf.at[own_column],
            p_send.at[side * w.nz + hop], p_recv.at[w.l * w.nz + hop], w.device(z=to, l=side),
        )

    def each_piece(side, action):
        for hop in range(w.nz):
            if hop:
                action(hop)
            else:
                pl.when(w.l != side)(functools.partial(action, hop))

    for side in range(w.nl):
        chunks = range(side * CHUNKS // w.nl, (side + 1) * CHUNKS // w.nl)
        for chunk in chunks:
            slope_gather.arrive(chunk, 2)
        if side == 0:
            for chunk in range(2, CHUNKS):
                slope_gather.forward(chunk, 2)
            if w.nl == 1:
                for chunk in range(2, CHUNKS):
                    slope_gather.arrive(chunk, 2)
        columns = pl.ds(side * side_width, side_width)
        total = dot(
            cols[...].reshape(w.nz * sub, plane * ROWS),
            s_buf[:, :, :, :, columns].reshape(plane * ROWS, side_width),
        )
        part_buf[side] = total.reshape(w.nz, sub, side_width)
        each_piece(side, lambda hop, side=side: p_copy(side, hop).start())
        if side == 0:
            small_c[w.c] = settle(y_copies(), small_y)
            for copy in c_copies():
                copy.start()

    small_d[dp] = settle(c_copies(), small_c)
    for copy in d_copies():
        copy.start()
    piece_buf[own_column] = part_buf[w.l, w.z]
    for chunk in range(CHUNKS):
        slope_gather.drain(chunk)
    for copy in z_copies() + y_copies() + c_copies():
        copy.wait_send()

    def p_wait(other, hop):
        at = ring(w.z, w.nz - hop, w.nz) * w.nl + other
        remote(
            piece_buf.at[at], piece_buf.at[at], p_send.at[other * w.nz + hop],
            p_recv.at[other * w.nz + hop], w.device(c=1 - w.c),
        ).wait_recv()

    for other in range(w.nl):
        each_piece(other, lambda hop, other=other: p_wait(other, hop))
    piece = piece_buf[0]
    for at in range(1, column):
        piece += piece_buf[at]
    squares = piece * piece
    narrow = squares[:, 0:128]
    for at in range(1, side_width // 128):
        narrow += squares[:, at * 128 : at * 128 + 128]
    sq_seq[me] = jnp.sum(narrow, axis=0, keepdims=True)

    def e_copy(hop):
        return remote(
            sq_seq.at[me], sq_seq.at[me], e_send.at[hop], e_recv.at[hop], (dp, ring(me, hop, ns))
        )

    def e_start(hop, _):
        e_copy(hop).start()
        return _

    def e_wait(hop, _):
        e_copy(hop).wait_recv()
        return _

    lax.fori_loop(1, ns, e_start, 0)
    full_buf[w.l, w.x] = piece

    def f_copy(hop):
        own = full_buf.at[w.l, w.x]
        return remote(own, own, f_send.at[hop], f_recv.at[hop], (ring(dp, hop, ndp), me))

    for hop in range(1, ndp):
        f_copy(hop).start()

    small = settle(d_copies(), small_d)
    second = small[0:HEADS, :]
    small_ref[0:HEADS, :] = second * inverse_root(whole_sum(second * second), HEADS * HIDDEN)
    first_bias = small[4:5, :]
    small_ref[4:5, :] = first_bias * inverse_root(whole_sum(first_bias * first_bias), HIDDEN)
    small_ref[5:6, :] = small[5:6, :]
    small_ref[8 : 8 + HEADS, 0:ROWS] = mass

    for side in range(w.nl):
        each_piece(side, lambda hop, side=side: p_copy(side, hop).wait_send())
    lax.fori_loop(1, ns, e_wait, 0)
    square = sq_seq[0]
    for at in range(1, ns):
        square += sq_seq[at]
    sq_dp[dp] = square

    def g_copy(hop):
        return remote(
            sq_dp.at[dp], sq_dp.at[dp], g_send.at[hop], g_recv.at[hop], (ring(dp, hop, ndp), me)
        )

    for hop in range(1, ndp):
        g_copy(hop).start()
    for hop in range(1, ndp):
        f_copy(hop).wait_recv()
    for hop in range(1, ndp):
        g_copy(hop).wait_recv()
    square = sq_dp[0]
    for at in range(1, ndp):
        square += sq_dp[at]
    scale = inverse_root(whole_sum(square), depth * HIDDEN)
    for side in range(w.nl):
        step_ref[:, side * side_width : (side + 1) * side_width] = (
            full_buf[side].reshape(wide, side_width) * scale
        )

    def e_drain(hop, _):
        e_copy(hop).wait_send()
        return _

    lax.fori_loop(1, ns, e_drain, 0)
    for copy in d_copies():
        copy.wait_send()
    for hop in range(1, ndp):
        f_copy(hop).wait_send()
        g_copy(hop).wait_send()


def finish(step_in, small_in, mass_ref, loss_ref, step_ref, second_ref, first_bias_ref, bias_ref):
    step_ref[...] = step_in[...]
    mass_ref[0] = small_in[8 : 8 + HEADS, 0:ROWS]
    loss_ref[...] = small_in[5:6, HEADS : HEADS + 1]
    second_ref[...] = small_in[0:HEADS, :]
    first_bias_ref[...] = small_in[4:5, :]
    bias_ref[...] = small_in[5:6, 0:HEADS]


def per_device(
    dp_parts, seq_parts, queries, key_rows, hidden, order, w1, b1, w2, b2
):
    f32, bf16 = jnp.float32, jnp.bfloat16
    (nl, nx), (ny, nz, nc) = dp_parts, seq_parts
    ns, ndp, plane, column = ny * nz * nc, nl * nx, nc * ny * nx, nz * nl
    depth = hidden.shape[2]
    wide = depth // ns
    sub, side_width = wide // nx, HIDDEN // nl
    vmem, smem, anywhere = (
        pl.BlockSpec(memory_space=pltpu.VMEM),
        pl.BlockSpec(memory_space=pltpu.SMEM),
        pl.BlockSpec(memory_space=pl.ANY),
    )
    dma = pltpu.SemaphoreType.DMA
    key_sems = [dma((CHUNKS, n)) for n in (nz, nz, ny, ny, 1, 1)]
    slope_sems = [dma((CHUNKS, max(nx, ny)))] * 4 + [dma((CHUNKS, 1))] * 2
    step, small = pl.pallas_call(
        functools.partial(kernel, dp_parts, seq_parts),
        out_shape=(
            jax.ShapeDtypeStruct((wide, HIDDEN), f32),
            jax.ShapeDtypeStruct((16, HIDDEN), f32),
        ),
        in_specs=[smem, smem, anywhere, anywhere, anywhere, anywhere, vmem, vmem],
        out_specs=(vmem,) * 2,
        scratch_shapes=[
            pltpu.VMEM((HEADS * GROUP * ROWS, HEAD_SIZE), bf16),
            pltpu.VMEM((HEADS, nc, ny, nz, ROWS, HEAD_SIZE), bf16),
            pltpu.VMEM((ROWS, depth), bf16),
            pltpu.VMEM((ny, nz, nc, nx, sub, ROWS), bf16),
            pltpu.VMEM((depth, HIDDEN), bf16),
            pltpu.VMEM((nc * ny, nz * ROWS, GROUP * ROWS), bf16),
            pltpu.VMEM((nc * ny, 8, GROUP * ROWS), f32),
            pltpu.VMEM((nz, sub, plane * ROWS), bf16),
            pltpu.VMEM((nc, ny, nx, ROWS, HIDDEN), bf16),
            pltpu.VMEM((ROWS, HIDDEN), f32),
            pltpu.VMEM((ROWS, HIDDEN), f32),
            pltpu.VMEM((ROWS, HIDDEN), bf16),
            pltpu.VMEM((ns, HEADS, ROWS), f32),
            pltpu.VMEM((ns, HEADS, ROWS), f32),
            pltpu.VMEM((nz, 8, HIDDEN), f32),
            pltpu.VMEM((ny, 8, HIDDEN), f32),
            pltpu.VMEM((nc, 8, HIDDEN), f32),
            pltpu.VMEM((ndp, 8, HIDDEN), f32),
            pltpu.VMEM((nl, nz, sub, side_width), f32),
            pltpu.VMEM((column, sub, side_width), f32),
            pltpu.VMEM((nl, nx, sub, side_width), f32),
            pltpu.VMEM((ns, 1, 128), f32),
            pltpu.VMEM((ndp, 1, 128), f32),
            dma((HEADS * GROUP,)), dma((HEADS,)), dma((1,)), dma((CHUNKS,)),
            *key_sems, *slope_sems,
            dma((plane,)), dma((plane,)), dma((ns,)), dma((ns,)),
            dma((nz,)), dma((nz,)), dma((ny,)), dma((ny,)), dma((nc,)), dma((nc,)),
            dma((ndp,)), dma((ndp,)), dma((column,)), dma((column,)), dma((ndp,)), dma((ndp,)),
            dma((ns,)), dma((ns,)), dma((ndp,)), dma((ndp,)),
        ],
        compiler_params=pltpu.CompilerParams(
            collective_id=0, has_side_effects=True, vmem_limit_bytes=60 * 1024 * 1024
        ),
    )(
        order, b2, queries.reshape(ROWS, -1), key_rows.reshape(ROWS, -1),
        hidden.reshape(ROWS, depth), w1, b1.reshape(1, HIDDEN), w2,
    )
    mass, loss, step, second, first_bias, bias = pl.pallas_call(
        finish,
        out_shape=(
            jax.ShapeDtypeStruct((1, HEADS, ROWS), f32),
            jax.ShapeDtypeStruct((1, 1), f32),
            jax.ShapeDtypeStruct((wide, HIDDEN), f32),
            jax.ShapeDtypeStruct((HEADS, HIDDEN), f32),
            jax.ShapeDtypeStruct((1, HIDDEN), f32),
            jax.ShapeDtypeStruct((1, HEADS), f32),
        ),
        in_specs=[vmem, vmem],
        out_specs=(vmem,) * 6,
    )(step, small)
    return (
        mass, loss.reshape(()), step, second, first_bias.reshape(HIDDEN), bias.reshape(HEADS)
    )


def solution(mesh, dp_parts=DP_PARTS, seq_parts=SEQ_PARTS):
    in_specs = (P("dp", "seq", None),) * 3 + (P(),) * 5
    out_specs = (P("dp", None, "seq"), P(), P("seq", None), P(), P(), P())
    body = functools.partial(per_device, dp_parts, seq_parts)
    return jax.shard_map(
        body, mesh=mesh, in_specs=in_specs, out_specs=out_specs, check_vma=False
    )
```

```python
import functools
import math

import jax
import jax.numpy as jnp
from jax import lax
from jax.experimental import pallas as pl
from jax.experimental.pallas import tpu as pltpu
from jax.sharding import PartitionSpec as P

MESH = pl.DeviceIdType.MESH
ROWS = 128
BLK = 64
HEAD_SIZE = 128
HEADS = 4
GROUP = 8
HIDDEN = 512
KEYS = 512
CHUNKS = 4
SCALE2 = HEAD_SIZE**-0.5 * math.log2(math.e)
LAST = (((1,), (1,)), ((), ()))
DP_PARTS = (2, 4)
SEQ_PARTS = (4, 4, 2)


def dot_t(a, b, precision=None):
    return lax.dot_general(a, b, LAST, preferred_element_type=jnp.float32, precision=precision)


def dot(a, b, precision=None):
    return jnp.dot(a, b, preferred_element_type=jnp.float32, precision=precision)


def ring(at, hop, size):
    return lax.rem(at + hop, size)


def remote(src, dst, send, recv, device):
    return pltpu.make_async_remote_copy(
        src_ref=src, dst_ref=dst, send_sem=send, recv_sem=recv, device_id=device,
        device_id_type=MESH,
    )


class Where:
    def __init__(self, dp_parts, seq_parts):
        self.nl, self.nx = dp_parts
        self.ny, self.nz, self.nc = seq_parts
        self.dp, self.seq = lax.axis_index("dp"), lax.axis_index("seq")
        self.x, self.l = lax.rem(self.dp, self.nx), self.dp // self.nx
        self.c = lax.rem(self.seq, self.nc)
        self.z = lax.rem(self.seq // self.nc, self.nz)
        self.y = self.seq // (self.nc * self.nz)

    def device(self, x=None, y=None, z=None, l=None, c=None):
        x, y, z, l, c = (
            own if given is None else given
            for given, own in zip((x, y, z, l, c), (self.x, self.y, self.z, self.l, self.c))
        )
        return (l * self.nx + x, (y * self.nz + z) * self.nc + c)


class Gather:
    def __init__(self, w, axis, view, y_first, sems):
        self.w, self.axis, self.view, self.sems, self.y_first = w, axis, view, sems, y_first
        self.b, self.nb = (w.z, w.nz) if axis == "z" else (w.x, w.nx)

    def copy(self, block, stage, chunk, device):
        send, recv = self.sems
        return remote(block, block, send.at[chunk, stage], recv.at[chunk, stage], device)

    def whole(self, chunk, stage):
        w = self.w
        y_step = stage == (0 if chunk in self.y_first else 1)
        if stage == 2:
            block = self.view(chunk, 1 - w.c)
        elif (w.ny if y_step else self.nb) == 1:
            return None
        elif y_step:
            rest = (self.b,) if stage == 0 else ()
            block = self.view(chunk, w.c, pl.ds(0, w.ny - 1), *rest)
        else:
            at_y = w.y if stage == 0 else slice(None)
            block = self.view(chunk, w.c, at_y, pl.ds(0, self.nb - 1))
        return self.copy(block, stage, chunk, w.device(c=1 - w.c))

    def sent(self, chunk, stage):
        w = self.w
        y_step = stage == (0 if chunk in self.y_first else 1)
        if stage == 2:
            return [(self.view(chunk, w.c), w.device(c=1 - w.c))]
        if stage == 0:
            block = self.view(chunk, w.c, w.y, self.b)
        elif y_step:
            block = self.view(chunk, w.c, w.y)
        else:
            block = self.view(chunk, w.c, slice(None), self.b)
        if y_step:
            return [(block, w.device(y=ring(w.y, hop, w.ny))) for hop in range(1, w.ny)]
        return [
            (block, w.device(**{self.axis: ring(self.b, hop, self.nb)}))
            for hop in range(1, self.nb)
        ]

    def start(self, chunk, stage):
        for block, device in self.sent(chunk, stage):
            self.copy(block, stage, chunk, device).start()

    def arrive(self, chunk, stage):
        whole = self.whole(chunk, stage)
        if whole is not None:
            whole.wait_recv()

    def forward(self, chunk, stage):
        self.arrive(chunk, stage - 1)
        self.start(chunk, stage)

    def drain(self, chunk):
        for stage in range(3):
            whole = self.whole(chunk, stage)
            if whole is not None:
                whole.wait_send()


def attend(head, order_ref, w, q_buf, k_buf, p_buf, m_buf, mass_out, before, middle):
    steps = w.nc * w.ny
    keys_here = w.nz * ROWS
    width = GROUP * ROWS
    lane = lax.broadcasted_iota(jnp.int32, (BLK, ROWS), 1)
    low, high = order_ref[2 * w.seq], order_ref[2 * w.seq + 1]
    q_pos = jnp.where(lane < BLK, low, high) * BLK + lax.rem(lane, BLK)
    inner = lax.broadcasted_iota(jnp.int32, (BLK, ROWS), 0)

    def visit(step, highest, summed):
        before(step)
        c, y = ring(w.c, step // w.ny, w.nc), ring(w.y, step % w.ny, w.ny)
        keys = k_buf[head, c, y].reshape(keys_here, HEAD_SIZE)
        pieces = []
        for part in range(keys_here // BLK):
            owner = (y * w.nz + part // 2) * w.nc + c
            k_pos = order_ref[2 * owner + part % 2] * BLK + inner
            pieces.append(jnp.where(k_pos <= q_pos, 0.0, -1e30))
        bias = jnp.concatenate(pieces, axis=0)
        bias = jnp.concatenate([bias, bias], axis=1)
        new_highest, new_summed = [], []
        for pair in range(GROUP // 2):
            start = pl.multiple_of((head * GROUP + 2 * pair) * ROWS, 2 * ROWS)
            score = dot_t(keys, q_buf[pl.ds(start, 2 * ROWS), :]) + bias
            old = highest[:, pair * 256 : pair * 256 + 256]
            top = jnp.maximum(old, jnp.max(score, axis=0, keepdims=True))
            weight = jnp.exp2((score - top) * SCALE2)
            total = summed[:, pair * 256 : pair * 256 + 256] * jnp.exp2((old - top) * SCALE2)
            new_highest.append(top)
            new_summed.append(total + jnp.sum(weight, axis=0, keepdims=True))
            p_buf[step, :, pair * 256 : pair * 256 + 256] = weight.astype(jnp.bfloat16)
        highest = jnp.concatenate(new_highest, axis=1)
        m_buf[step, 0:1, :] = highest
        return highest, jnp.concatenate(new_summed, axis=1)

    highest, summed = jnp.full((1, width), -1e30, jnp.float32), jnp.zeros((1, width), jnp.float32)
    for step in range(steps):
        highest, summed = visit(step, highest, summed)
    middle()
    inverse = 1.0 / (summed * GROUP)
    row = lax.broadcasted_iota(jnp.int32, (16, width), 0)

    for step in range(steps):
        scale = jnp.exp2((m_buf[step, 0:1, :] - highest) * SCALE2) * inverse
        coarse = scale.astype(jnp.bfloat16).astype(jnp.float32)
        both = jnp.where(row == 0, coarse, jnp.where(row == 1, scale - coarse, 0.0))
        mass = dot_t(both.astype(jnp.bfloat16), p_buf[step])
        line = mass[0:1, :] + mass[1:2, :]
        c, y = ring(w.c, step // w.ny, w.nc), ring(w.y, step % w.ny, w.ny)
        for part in range(w.nz):
            mass_out[(y * w.nz + part) * w.nc + c, pl.ds(head, 1), :] = line[
                :, part * ROWS : part * ROWS + ROWS
            ]


def inverse_root(square_sum, entries):
    return 1.0 / jnp.sqrt(square_sum / entries + 1e-06)


def whole_sum(x):
    return jnp.sum(jnp.sum(x, axis=1, keepdims=True), axis=0, keepdims=True)


def kernel(
    dp_parts, seq_parts,
    order_ref, b2_ref, q_hbm, k_hbm, hs_hbm, w1_hbm, b1_ref, w2_ref,
    step_ref, small_ref,
    q_buf, k_buf, hs_buf, turned, w1_buf, p_buf, m_buf, cols, s_buf, pre_buf, gate_buf, hid_buf,
    mass_out, mass_in, small_z, small_y, small_c, small_d,
    part_buf, piece_buf, full_buf, sq_seq, sq_dp,
    q_sem, k_sem, hs_sem, w1_sem,
    kg_send, kg_recv, sg_send, sg_recv,
    a_send, a_recv, m_send, m_recv, z_send, z_recv, y_send, y_recv, c_send, c_recv,
    d_send, d_recv, p_send, p_recv, f_send, f_recv, e_send, e_recv, g_send, g_recv,
):
    w = Where(dp_parts, seq_parts)
    ns, ndp, plane = w.ny * w.nz * w.nc, w.nl * w.nx, w.nc * w.ny * w.nx
    me, dp = w.seq, w.dp
    length = float(ns * ROWS)
    depth = hs_hbm.shape[1]
    wide = depth // ns
    sub = wide // w.nx
    side_width = HIDDEN // w.nl

    def key_view(chunk, *at):
        return k_buf.at[(chunk, *at)]

    def slope_view(chunk, *at):
        at = at + (slice(None),) * (4 - len(at))
        return s_buf.at[(*at, pl.ds(chunk * 128, 128))]

    def all_of(ref, send, recv):
        return remote(ref, ref, send.at[0], recv.at[0], w.device(c=1 - w.c))

    key_gather = Gather(w, "z", key_view, (), (kg_send, kg_recv))
    slope_gather = Gather(w, "x", slope_view, (1, 3), (sg_send, sg_recv))

    k_copies = [
        pltpu.make_async_copy(
            k_hbm.at[:, pl.ds(head * HEAD_SIZE, HEAD_SIZE)], key_view(head, w.c, w.y, w.z),
            k_sem.at[0],
        )
        for head in range(HEADS)
    ]
    for copy in k_copies:
        copy.start()

    barrier = pltpu.get_barrier_semaphore()

    def greet(device):
        pl.semaphore_signal(barrier, inc=1, device_id=device, device_id_type=MESH)

    def greet_seq(hop, _):
        greet((dp, ring(me, hop, ns)))
        return _

    def in_plane(index):
        return lax.rem(index, w.nx), lax.rem(index // w.nx, w.ny), index // (w.nx * w.ny)

    own_plane = (w.c * w.ny + w.y) * w.nx + w.x

    def plane_device(hop):
        x, y, c = in_plane(ring(own_plane, hop, plane))
        return w.device(x=x, y=y, c=c)

    def greet_plane(hop, _):
        greet(plane_device(hop))
        return _

    def greet_dp(hop, _):
        greet((ring(dp, hop, ndp), me))
        return _

    own_column = w.z * w.nl + w.l
    column = w.nz * w.nl

    def greet_column(hop, _):
        at = ring(own_column, hop, column)
        greet(w.device(z=at // w.nl, l=lax.rem(at, w.nl)))
        return _

    lax.fori_loop(1, ns, greet_seq, 0)
    lax.fori_loop(1, plane, greet_plane, 0)
    lax.fori_loop(1, ndp, greet_dp, 0)
    lax.fori_loop(1, column, greet_column, 0)

    quarters = CHUNKS
    span = depth // quarters

    def w1_copy(quarter):
        return pltpu.make_async_copy(
            w1_hbm.at[pl.ds(quarter * span, span), :], w1_buf.at[pl.ds(quarter * span, span), :],
            w1_sem.at[quarter],
        )

    hs_copy = pltpu.make_async_copy(hs_hbm, hs_buf, hs_sem.at[0])
    hs_copy.start()
    for quarter in range(quarters):
        w1_copy(quarter).start()

    def q_copy(head):
        return pltpu.make_async_copy(
            q_hbm.at[:, pl.ds(pl.multiple_of(head * HEAD_SIZE, 128), HEAD_SIZE)],
            q_buf.at[pl.ds(pl.multiple_of(head * ROWS, ROWS), ROWS), :],
            q_sem.at[0],
        )

    def q_start(head, _):
        q_copy(head).start()
        return _

    lax.fori_loop(0, HEADS * GROUP, q_start, 0)

    tiles = 128 // math.gcd(sub, 128)
    rows_of = min(sub, 128)

    def turn(tile, _):
        value = jnp.transpose(hs_buf[:, pl.ds(pl.multiple_of(tile * 128, 128), 128)])
        block, inside = tile // (wide // 128), lax.rem(tile, wide // 128)
        c = lax.rem(block, w.nc)
        z = lax.rem(block // w.nc, w.nz)
        y = block // (w.nc * w.nz)
        if sub <= 128:
            turned[y, z, c, pl.ds(inside * tiles, tiles)] = value.reshape(tiles, rows_of, ROWS)
        else:
            per = sub // 128
            start = pl.multiple_of(lax.rem(inside, per) * 128, 128)
            turned[y, z, c, inside // per, pl.ds(start, 128), :] = value
        return _

    own_keys = k_buf.at[:, w.c, w.y, w.z]
    pltpu.make_async_copy(own_keys, own_keys, k_sem.at[0]).wait()
    pl.semaphore_wait(barrier, ns - 1 + plane - 1 + ndp - 1 + column - 1)
    key_gather.start(0, 0)
    hs_copy.wait()

    pre_buf[...] = jnp.broadcast_to(b1_ref[...], (ROWS, HIDDEN))
    per_quarter = depth // 128 // quarters
    deep = min(1024, span)
    for quarter in range(quarters):
        w1_copy(quarter).wait()

        def project(tile, _):
            at = pl.multiple_of(quarter * span + tile * deep, deep)
            pre_buf[...] += dot(hs_buf[:, pl.ds(at, deep)], w1_buf[pl.ds(at, deep), :])
            return _

        lax.fori_loop(0, span // deep, project, 0)
        lax.fori_loop(quarter * per_quarter, (quarter + 1) * per_quarter, turn, 0)
        if quarter:
            key_gather.forward(quarter - 1, 1)
        if quarter + 1 < CHUNKS:
            key_gather.start(quarter + 1, 0)

    pre = pre_buf[...]
    gate = 1.0 / (1.0 + jnp.exp(-pre))
    gate_buf[...] = gate * (1.0 + pre * (1.0 - gate))
    hid_buf[...] = (pre * gate).astype(jnp.bfloat16)

    own_cols = cols.at[:, :, pl.ds(pl.multiple_of(own_plane * ROWS, ROWS), ROWS)]

    def a_copy(hop):
        x, y, c = in_plane(ring(own_plane, hop, plane))
        return remote(
            turned.at[y, :, c, x], own_cols, a_send.at[0], a_recv.at[0],
            w.device(x=x, y=y, c=c),
        )

    def a_start(hop, _):
        a_copy(hop).start()
        return _

    pltpu.make_async_copy(q_buf, q_buf, q_sem.at[0]).wait()
    cols[:, :, pl.ds(pl.multiple_of(own_plane * ROWS, ROWS), ROWS)] = turned[w.y, :, w.c, w.x]

    def first_steps(step):
        if step == 1:
            key_gather.forward(CHUNKS - 1, 1)
            key_gather.forward(0, 2)
        if step == w.ny:
            key_gather.arrive(0, 2)

    attend(
        0, order_ref, w, q_buf, k_buf, p_buf, m_buf, mass_out, first_steps,
        lambda: key_gather.forward(1, 2),
    )

    def one_head(head, _):
        def middle():
            @pl.when(head < HEADS - 1)
            def _():
                key_gather.forward(head + 1, 2)

            @pl.when(head == 1)
            def _():
                lax.fori_loop(1, plane, a_start, 0)

        key_gather.arrive(head, 2)
        attend(
            head, order_ref, w, q_buf, k_buf, p_buf, m_buf, mass_out, lambda step: None, middle
        )
        return _

    lax.fori_loop(1, HEADS, one_head, 0)

    def m_copy(hop):
        to = ring(me, hop, ns)
        return remote(mass_out.at[to], mass_in.at[hop - 1], m_send.at[0], m_recv.at[0], (dp, to))

    def m_start(hop, _):
        m_copy(hop).start()
        return _

    lax.fori_loop(1, ns, m_start, 0)
    predicted = dot_t(w2_ref[...], hid_buf[...])
    line = lax.broadcasted_iota(jnp.int32, (HEADS, ROWS), 0)
    for head in range(HEADS):
        predicted += jnp.where(line == head, b2_ref[head], 0.0)

    for chunk in range(CHUNKS):
        key_gather.drain(chunk)

    all_of(mass_in.at[pl.ds(0, ns - 1)], m_send, m_recv).wait_recv()
    mass = mass_out[me]
    for at in range(ns - 1):
        mass += mass_in[at]
    residue = predicted - jnp.log(1.0 + mass)
    out_grad = residue / length
    turned_grad = jnp.transpose(
        jnp.concatenate([out_grad, jnp.zeros((8 - HEADS, ROWS), jnp.float32)], axis=0)
    )
    w2_wide = w2_ref[...].astype(jnp.float32)
    back = turned_grad[:, 0:1] * w2_wide[0:1, :]
    for head in range(1, HEADS):
        back += turned_grad[:, head : head + 1] * w2_wide[head : head + 1, :]
    slope = back * gate_buf[...]
    s_buf[w.c, w.y, w.x] = slope.astype(jnp.bfloat16)
    for chunk in range(CHUNKS):
        slope_gather.start(chunk, 0)

    def exchange(buf, at, count, send, recv, device):
        return [
            remote(buf.at[at], buf.at[at], send.at[0], recv.at[0], device(hop))
            for hop in range(1, count)
        ]

    def z_copies():
        return exchange(
            small_z, w.z, w.nz, z_send, z_recv, lambda hop: w.device(z=ring(w.z, hop, w.nz))
        )

    def y_copies():
        return exchange(
            small_y, w.y, w.ny, y_send, y_recv, lambda hop: w.device(y=ring(w.y, hop, w.ny))
        )

    def c_copies():
        return exchange(small_c, w.c, w.nc, c_send, c_recv, lambda hop: w.device(c=1 - w.c))

    def d_copies():
        return exchange(small_d, dp, ndp, d_send, d_recv, lambda hop: (ring(dp, hop, ndp), me))

    def settle(buf, send, recv):
        if buf.shape[0] > 1:
            all_of(buf.at[pl.ds(0, buf.shape[0] - 1)], send, recv).wait_recv()
        total = buf[0]
        for at in range(1, buf.shape[0]):
            total += buf[at]
        return total

    exact = lax.Precision.HIGHEST
    second = dot(out_grad, hid_buf[...].astype(jnp.float32), exact)
    first_bias = jnp.sum(slope, axis=0, keepdims=True)
    place = lax.broadcasted_iota(jnp.int32, (1, HIDDEN), 1)
    bias_sum = jnp.sum(out_grad, axis=1, keepdims=True)
    loss = 0.5 * whole_sum(residue * residue)
    last = jnp.where(place == HEADS, loss / length, 0.0)
    for head in range(HEADS):
        last = jnp.where(place == head, bias_sum[head : head + 1, :], last)
    small_z[w.z] = jnp.concatenate(
        [second, first_bias, last, jnp.zeros((2, HIDDEN), jnp.float32)], axis=0
    )
    for copy in z_copies():
        copy.start()

    all_of(mass_in.at[pl.ds(0, ns - 1)], m_send, m_recv).wait_send()
    for chunk in range(CHUNKS):
        slope_gather.forward(chunk, 1)
    small_y[w.y] = settle(small_z, z_send, z_recv)
    for copy in y_copies():
        copy.start()
    slope_gather.forward(0, 2)
    slope_gather.forward(1, 2)

    all_of(cols.at[:, :, pl.ds(0, (plane - 1) * ROWS)], a_send, a_recv).wait()

    def p_copy(side, hop):
        to = ring(w.z, hop, w.nz)
        return remote(
            part_buf.at[side, to], piece_buf.at[own_column],
            p_send.at[0], p_recv.at[0], w.device(z=to, l=side),
        )

    def each_piece(side, action):
        for hop in range(w.nz):
            if hop:
                action(hop)
            else:
                pl.when(w.l != side)(functools.partial(action, hop))

    for side in range(w.nl):
        chunks = range(side * CHUNKS // w.nl, (side + 1) * CHUNKS // w.nl)
        for chunk in chunks:
            if chunk >= 2:
                slope_gather.forward(chunk, 2)
        for chunk in chunks:
            slope_gather.arrive(chunk, 2)
        columns = pl.ds(side * side_width, side_width)
        total = dot(
            cols[...].reshape(w.nz * sub, plane * ROWS),
            s_buf[:, :, :, :, columns].reshape(plane * ROWS, side_width),
        )
        part_buf[side] = total.reshape(w.nz, sub, side_width)
        each_piece(side, lambda hop, side=side: p_copy(side, hop).start())
        if side == 0:
            small_c[w.c] = settle(small_y, y_send, y_recv)
            for copy in c_copies():
                copy.start()

    small_d[dp] = settle(small_c, c_send, c_recv)
    for copy in d_copies():
        copy.start()
    piece_buf[own_column] = part_buf[w.l, w.z]
    for chunk in range(CHUNKS):
        slope_gather.drain(chunk)
    for buf, send, recv in (
        (small_z, z_send, z_recv), (small_y, y_send, y_recv), (small_c, c_send, c_recv)
    ):
        if buf.shape[0] > 1:
            all_of(buf.at[pl.ds(0, buf.shape[0] - 1)], send, recv).wait_send()

    all_of(piece_buf.at[pl.ds(0, column - 1)], p_send, p_recv).wait_recv()
    piece = piece_buf[0]
    for at in range(1, column):
        piece += piece_buf[at]
    squares = piece * piece
    narrow = squares[:, 0:128]
    for at in range(1, side_width // 128):
        narrow += squares[:, at * 128 : at * 128 + 128]
    sq_seq[me] = jnp.sum(narrow, axis=0, keepdims=True)

    def e_copy(hop):
        return remote(
            sq_seq.at[me], sq_seq.at[me], e_send.at[0], e_recv.at[0], (dp, ring(me, hop, ns))
        )

    def e_start(hop, _):
        e_copy(hop).start()
        return _

    lax.fori_loop(1, ns, e_start, 0)
    full_buf[dp] = piece

    def f_copy(hop):
        own = full_buf.at[dp]
        return remote(own, own, f_send.at[0], f_recv.at[0], (ring(dp, hop, ndp), me))

    for hop in range(1, ndp):
        f_copy(hop).start()

    small = settle(small_d, d_send, d_recv)
    second = small[0:HEADS, :]
    small_ref[0:HEADS, :] = second * inverse_root(whole_sum(second * second), HEADS * HIDDEN)
    first_bias = small[4:5, :]
    small_ref[4:5, :] = first_bias * inverse_root(whole_sum(first_bias * first_bias), HIDDEN)
    small_ref[5:6, :] = small[5:6, :]
    small_ref[8 : 8 + HEADS, 0:ROWS] = mass

    all_of(piece_buf.at[pl.ds(0, column - 1)], p_send, p_recv).wait_send()
    all_of(sq_seq.at[pl.ds(0, ns - 1)], e_send, e_recv).wait_recv()
    square = sq_seq[0]
    for at in range(1, ns):
        square += sq_seq[at]
    sq_dp[dp] = square

    def g_copy(hop):
        return remote(
            sq_dp.at[dp], sq_dp.at[dp], g_send.at[0], g_recv.at[0], (ring(dp, hop, ndp), me)
        )

    for hop in range(1, ndp):
        g_copy(hop).start()
    all_of(full_buf.at[pl.ds(0, ndp - 1)], f_send, f_recv).wait_recv()
    all_of(sq_dp.at[pl.ds(0, ndp - 1)], g_send, g_recv).wait_recv()
    square = sq_dp[0]
    for at in range(1, ndp):
        square += sq_dp[at]
    scale = inverse_root(whole_sum(square), depth * HIDDEN)
    for side in range(w.nl):
        step_ref[:, side * side_width : (side + 1) * side_width] = (
            full_buf[side * w.nx : (side + 1) * w.nx].reshape(wide, side_width) * scale
        )

    all_of(sq_seq.at[pl.ds(0, ns - 1)], e_send, e_recv).wait_send()
    all_of(small_d.at[pl.ds(0, ndp - 1)], d_send, d_recv).wait_send()
    all_of(full_buf.at[pl.ds(0, ndp - 1)], f_send, f_recv).wait_send()
    all_of(sq_dp.at[pl.ds(0, ndp - 1)], g_send, g_recv).wait_send()


def finish(step_in, small_in, mass_ref, loss_ref, step_ref, second_ref, first_bias_ref, bias_ref):
    step_ref[...] = step_in[...]
    mass_ref[0] = small_in[8 : 8 + HEADS, 0:ROWS]
    loss_ref[...] = small_in[5:6, HEADS : HEADS + 1]
    second_ref[...] = small_in[0:HEADS, :]
    first_bias_ref[...] = small_in[4:5, :]
    bias_ref[...] = small_in[5:6, 0:HEADS]


def per_device(
    dp_parts, seq_parts, queries, key_rows, hidden, order, w1, b1, w2, b2
):
    f32, bf16 = jnp.float32, jnp.bfloat16
    (nl, nx), (ny, nz, nc) = dp_parts, seq_parts
    ns, ndp, plane, column = ny * nz * nc, nl * nx, nc * ny * nx, nz * nl
    depth = hidden.shape[2]
    wide = depth // ns
    sub, side_width = wide // nx, HIDDEN // nl
    vmem, smem, anywhere = (
        pl.BlockSpec(memory_space=pltpu.VMEM),
        pl.BlockSpec(memory_space=pltpu.SMEM),
        pl.BlockSpec(memory_space=pl.ANY),
    )
    dma = pltpu.SemaphoreType.DMA
    step, small = pl.pallas_call(
        functools.partial(kernel, dp_parts, seq_parts),
        out_shape=(
            jax.ShapeDtypeStruct((wide, HIDDEN), f32),
            jax.ShapeDtypeStruct((16, HIDDEN), f32),
        ),
        in_specs=[smem, smem, anywhere, anywhere, anywhere, anywhere, vmem, vmem],
        out_specs=(vmem,) * 2,
        scratch_shapes=[
            pltpu.VMEM((HEADS * GROUP * ROWS, HEAD_SIZE), bf16),
            pltpu.VMEM((HEADS, nc, ny, nz, ROWS, HEAD_SIZE), bf16),
            pltpu.VMEM((ROWS, depth), bf16),
            pltpu.VMEM((ny, nz, nc, nx, sub, ROWS), bf16),
            pltpu.VMEM((depth, HIDDEN), bf16),
            pltpu.VMEM((nc * ny, nz * ROWS, GROUP * ROWS), bf16),
            pltpu.VMEM((nc * ny, 8, GROUP * ROWS), f32),
            pltpu.VMEM((nz, sub, plane * ROWS), bf16),
            pltpu.VMEM((nc, ny, nx, ROWS, HIDDEN), bf16),
            pltpu.VMEM((ROWS, HIDDEN), f32),
            pltpu.VMEM((ROWS, HIDDEN), f32),
            pltpu.VMEM((ROWS, HIDDEN), bf16),
            pltpu.VMEM((ns, HEADS, ROWS), f32),
            pltpu.VMEM((ns, HEADS, ROWS), f32),
            pltpu.VMEM((nz, 8, HIDDEN), f32),
            pltpu.VMEM((ny, 8, HIDDEN), f32),
            pltpu.VMEM((nc, 8, HIDDEN), f32),
            pltpu.VMEM((ndp, 8, HIDDEN), f32),
            pltpu.VMEM((nl, nz, sub, side_width), f32),
            pltpu.VMEM((column, sub, side_width), f32),
            pltpu.VMEM((ndp, sub, side_width), f32),
            pltpu.VMEM((ns, 1, 128), f32),
            pltpu.VMEM((ndp, 1, 128), f32),
            dma((1,)), dma((1,)), dma((1,)), dma((CHUNKS,)),
            *[dma((CHUNKS, 3))] * 4, *[dma((1,))] * 20,
        ],
        compiler_params=pltpu.CompilerParams(
            collective_id=0, has_side_effects=True, vmem_limit_bytes=60 * 1024 * 1024
        ),
    )(
        order, b2, queries.reshape(ROWS, -1), key_rows.reshape(ROWS, -1),
        hidden.reshape(ROWS, depth), w1, b1.reshape(1, HIDDEN), w2,
    )
    mass, loss, step, second, first_bias, bias = pl.pallas_call(
        finish,
        out_shape=(
            jax.ShapeDtypeStruct((1, HEADS, ROWS), f32),
            jax.ShapeDtypeStruct((1, 1), f32),
            jax.ShapeDtypeStruct((wide, HIDDEN), f32),
            jax.ShapeDtypeStruct((HEADS, HIDDEN), f32),
            jax.ShapeDtypeStruct((1, HIDDEN), f32),
            jax.ShapeDtypeStruct((1, HEADS), f32),
        ),
        in_specs=[vmem, vmem],
        out_specs=(vmem,) * 6,
    )(step, small)
    return (
        mass, loss.reshape(()), step, second, first_bias.reshape(HIDDEN), bias.reshape(HEADS)
    )


def solution(mesh, dp_parts=DP_PARTS, seq_parts=SEQ_PARTS):
    in_specs = (P("dp", "seq", None),) * 3 + (P(),) * 5
    out_specs = (P("dp", None, "seq"), P(), P("seq", None), P(), P(), P())
    body = functools.partial(per_device, dp_parts, seq_parts)
    return jax.shard_map(
        body, mesh=mesh, in_specs=in_specs, out_specs=out_specs, check_vma=False
    )
```

```python
import functools
import math

import jax
import jax.numpy as jnp
from jax import lax
from jax.experimental import pallas as pl
from jax.experimental.pallas import tpu as pltpu
from jax.sharding import PartitionSpec as P

MESH = pl.DeviceIdType.MESH
ROWS = 128
BLK = 64
HEAD_SIZE = 128
HEADS = 4
GROUP = 8
HIDDEN = 512
KEYS = 512
CHUNKS = 4
HIDE = -32768.0
SCALE2 = HEAD_SIZE**-0.5 * math.log2(math.e)
LAST = (((1,), (1,)), ((), ()))
DP_PARTS = (2, 4)
SEQ_PARTS = (4, 4, 2)


def dot_t(a, b, precision=None):
    return lax.dot_general(a, b, LAST, preferred_element_type=jnp.float32, precision=precision)


def dot(a, b, precision=None):
    return jnp.dot(a, b, preferred_element_type=jnp.float32, precision=precision)


def ring(at, hop, size):
    return lax.rem(at + hop, size)


def remote(src, dst, send, recv, device):
    return pltpu.make_async_remote_copy(
        src_ref=src, dst_ref=dst, send_sem=send, recv_sem=recv, device_id=device,
        device_id_type=MESH,
    )


class Where:
    def __init__(self, dp_parts, seq_parts):
        self.nl, self.nx = dp_parts
        self.ny, self.nz, self.nc = seq_parts
        self.dp, self.seq = lax.axis_index("dp"), lax.axis_index("seq")
        self.x, self.l = lax.rem(self.dp, self.nx), self.dp // self.nx
        self.c = lax.rem(self.seq, self.nc)
        self.z = lax.rem(self.seq // self.nc, self.nz)
        self.y = self.seq // (self.nc * self.nz)

    def device(self, x=None, y=None, z=None, l=None, c=None):
        x, y, z, l, c = (
            own if given is None else given
            for given, own in zip((x, y, z, l, c), (self.x, self.y, self.z, self.l, self.c))
        )
        return (l * self.nx + x, (y * self.nz + z) * self.nc + c)


class Gather:
    def __init__(self, w, axis, view, y_first, sems):
        self.w, self.axis, self.view, self.sems, self.y_first = w, axis, view, sems, y_first
        self.b, self.nb = (w.z, w.nz) if axis == "z" else (w.x, w.nx)

    def copy(self, block, stage, chunk, device):
        send, recv = self.sems
        return remote(block, block, send.at[chunk, stage], recv.at[chunk, stage], device)

    def whole(self, chunk, stage):
        w = self.w
        if stage == 2:
            return self.copy(self.view(chunk, 1 - w.c), stage, chunk, w.device(c=1 - w.c))
        y_step = stage == (0 if chunk in self.y_first else 1)
        if (w.ny if y_step else self.nb) == 1:
            return None
        elif y_step:
            rest = (self.b,) if stage == 0 else ()
            block = self.view(chunk, w.c, pl.ds(0, w.ny - 1), *rest)
        else:
            at_y = w.y if stage == 0 else slice(None)
            block = self.view(chunk, w.c, at_y, pl.ds(0, self.nb - 1))
        return self.copy(block, stage, chunk, w.device(c=1 - w.c))

    def sent(self, chunk, stage):
        w = self.w
        y_step = stage == (0 if chunk in self.y_first else 1)
        if stage == 2:
            return [(self.view(chunk, w.c), w.device(c=1 - w.c))]
        if stage == 0:
            block = self.view(chunk, w.c, w.y, self.b)
        elif y_step:
            block = self.view(chunk, w.c, w.y)
        else:
            block = self.view(chunk, w.c, slice(None), self.b)
        if y_step:
            return [(block, w.device(y=ring(w.y, hop, w.ny))) for hop in range(1, w.ny)]
        return [
            (block, w.device(**{self.axis: ring(self.b, hop, self.nb)}))
            for hop in range(1, self.nb)
        ]

    def start(self, chunk, stage):
        for block, device in self.sent(chunk, stage):
            self.copy(block, stage, chunk, device).start()

    def arrive(self, chunk, stage):
        whole = self.whole(chunk, stage)
        if whole is not None:
            whole.wait_recv()

    def forward(self, chunk, stage):
        self.arrive(chunk, stage - 1)
        self.start(chunk, stage)

    def drain(self, chunk):
        for stage in range(3):
            whole = self.whole(chunk, stage)
            if whole is not None:
                whole.wait_send()


def attend(
    head, order_ref, w, q_buf, k_buf, hide_buf, side_buf, p_buf, m_buf, mass_out, before, middle
):
    steps = w.nc * w.ny
    keys_here = w.nz * ROWS
    width = GROUP * ROWS
    lane = lax.broadcasted_iota(jnp.int32, (BLK, ROWS), 1)
    low, high = order_ref[2 * w.seq], order_ref[2 * w.seq + 1]
    q_pos = jnp.where(lane < BLK, low, high) * BLK + lax.rem(lane, BLK)
    inner = lax.broadcasted_iota(jnp.int32, (BLK, ROWS), 0)

    def visit(step, highest, summed):
        before(step)
        c, y = ring(w.c, step // w.ny, w.nc), ring(w.y, step % w.ny, w.ny)
        keys = k_buf[head, c, y].reshape(keys_here, HEAD_SIZE)
        if step == 0:
            pieces = []
            for part in range(keys_here // BLK):
                owner = (y * w.nz + part // 2) * w.nc + c
                k_pos = order_ref[2 * owner + part % 2] * BLK + inner
                pieces.append(jnp.where(k_pos <= q_pos, 0.0, -1e30))
            bias = jnp.concatenate(pieces, axis=0)
            bias = jnp.concatenate([bias, bias], axis=1)
        else:
            keys = jnp.concatenate([keys, hide_buf[step]], axis=1)
        new_highest, new_summed = [], []
        for pair in range(GROUP // 2):
            start = pl.multiple_of((head * GROUP + 2 * pair) * ROWS, 2 * ROWS)
            queries = q_buf[pl.ds(start, 2 * ROWS), :]
            if step == 0:
                score = dot_t(keys, queries) + bias
            else:
                score = dot_t(keys, jnp.concatenate([queries, side_buf[...]], axis=1))
            old = highest[:, pair * 256 : pair * 256 + 256]
            top = jnp.maximum(old, jnp.max(score, axis=0, keepdims=True))
            weight = jnp.exp2((score - top) * SCALE2)
            total = summed[:, pair * 256 : pair * 256 + 256] * jnp.exp2((old - top) * SCALE2)
            new_highest.append(top)
            new_summed.append(total + jnp.sum(weight, axis=0, keepdims=True))
            p_buf[step, :, pair * 256 : pair * 256 + 256] = weight.astype(jnp.bfloat16)
        highest = jnp.concatenate(new_highest, axis=1)
        m_buf[step, 0:1, :] = highest
        return highest, jnp.concatenate(new_summed, axis=1)

    highest, summed = jnp.full((1, width), -1e30, jnp.float32), jnp.zeros((1, width), jnp.float32)
    for step in range(steps):
        highest, summed = visit(step, highest, summed)
    middle()
    inverse = 1.0 / (summed * GROUP)
    row = lax.broadcasted_iota(jnp.int32, (16, width), 0)

    for step in range(steps):
        scale = jnp.exp2((m_buf[step, 0:1, :] - highest) * SCALE2) * inverse
        coarse = scale.astype(jnp.bfloat16).astype(jnp.float32)
        both = jnp.where(row == 0, coarse, jnp.where(row == 1, scale - coarse, 0.0))
        mass = dot_t(both.astype(jnp.bfloat16), p_buf[step])
        line = mass[0:1, :] + mass[1:2, :]
        c, y = ring(w.c, step // w.ny, w.nc), ring(w.y, step % w.ny, w.ny)
        for part in range(w.nz):
            mass_out[(y * w.nz + part) * w.nc + c, pl.ds(head, 1), :] = line[
                :, part * ROWS : part * ROWS + ROWS
            ]


def inverse_root(square_sum, entries):
    return 1.0 / jnp.sqrt(square_sum / entries + 1e-06)


def whole_sum(x):
    return jnp.sum(jnp.sum(x, axis=1, keepdims=True), axis=0, keepdims=True)


def kernel(
    dp_parts, seq_parts,
    order_ref, b2_ref, q_hbm, k_hbm, hs_hbm, w1_hbm, b1_ref, w2_ref,
    step_ref, small_ref,
    q_buf, k_buf, hide_buf, side_buf, hs_buf, turned, w1_buf, p_buf, m_buf, cols, s_buf, pre_buf, gate_buf, hid_buf,
    mass_out, mass_in, small_z, small_y, small_c, small_d,
    part_buf, piece_buf, full_buf, sq_seq, sq_dp,
    q_sem, k_sem, hs_sem, w1_sem,
    kg_send, kg_recv, sg_send, sg_recv,
    a_send, a_recv, m_send, m_recv, z_send, z_recv, y_send, y_recv, c_send, c_recv,
    d_send, d_recv, p_send, p_recv, f_send, f_recv, e_send, e_recv, g_send, g_recv,
):
    w = Where(dp_parts, seq_parts)
    ns, ndp, plane = w.ny * w.nz * w.nc, w.nl * w.nx, w.nc * w.ny * w.nx
    me, dp = w.seq, w.dp
    length = float(ns * ROWS)
    depth = hs_hbm.shape[1]
    wide = depth // ns
    sub = wide // w.nx
    side_width = HIDDEN // w.nl

    def key_view(chunk, *at):
        return k_buf.at[(chunk, *at)]

    def slope_view(chunk, *at):
        at = at + (slice(None),) * (4 - len(at))
        return s_buf.at[(*at, pl.ds(chunk * 128, 128))]

    def all_of(ref, send, recv):
        return remote(ref, ref, send.at[0], recv.at[0], w.device(c=1 - w.c))

    key_gather = Gather(w, "z", key_view, (CHUNKS - 1,), (kg_send, kg_recv))
    slope_gather = Gather(w, "x", slope_view, (1, 3), (sg_send, sg_recv))

    k_copies = [
        pltpu.make_async_copy(
            k_hbm.at[:, pl.ds(head * HEAD_SIZE, HEAD_SIZE)], key_view(head, w.c, w.y, w.z),
            k_sem.at[0],
        )
        for head in range(HEADS)
    ]
    for copy in k_copies:
        copy.start()

    barrier = pltpu.get_barrier_semaphore()

    def greet(device):
        pl.semaphore_signal(barrier, inc=1, device_id=device, device_id_type=MESH)

    def greet_seq(hop, _):
        greet((dp, ring(me, hop, ns)))
        return _

    def in_plane(index):
        return lax.rem(index, w.nx), lax.rem(index // w.nx, w.ny), index // (w.nx * w.ny)

    own_plane = (w.c * w.ny + w.y) * w.nx + w.x

    def plane_device(hop):
        x, y, c = in_plane(ring(own_plane, hop, plane))
        return w.device(x=x, y=y, c=c)

    def greet_plane(hop, _):
        greet(plane_device(hop))
        return _

    def greet_dp(hop, _):
        greet((ring(dp, hop, ndp), me))
        return _

    own_column = w.z * w.nl + w.l
    column = w.nz * w.nl

    def greet_column(hop, _):
        at = ring(own_column, hop, column)
        greet(w.device(z=at // w.nl, l=lax.rem(at, w.nl)))
        return _

    lax.fori_loop(1, ns, greet_seq, 0)
    lax.fori_loop(1, plane, greet_plane, 0)
    lax.fori_loop(1, ndp, greet_dp, 0)
    lax.fori_loop(1, column, greet_column, 0)

    quarters = CHUNKS
    span = depth // quarters

    def w1_copy(quarter):
        return pltpu.make_async_copy(
            w1_hbm.at[pl.ds(quarter * span, span), :], w1_buf.at[pl.ds(quarter * span, span), :],
            w1_sem.at[quarter],
        )

    hs_copy = pltpu.make_async_copy(hs_hbm, hs_buf, hs_sem.at[0])
    hs_copy.start()
    for quarter in range(quarters):
        w1_copy(quarter).start()

    def q_copy(head):
        return pltpu.make_async_copy(
            q_hbm.at[:, pl.ds(pl.multiple_of(head * HEAD_SIZE, 128), HEAD_SIZE)],
            q_buf.at[pl.ds(pl.multiple_of(head * ROWS, ROWS), ROWS), :],
            q_sem.at[0],
        )

    def q_start(head, _):
        q_copy(head).start()
        return _

    lax.fori_loop(0, HEADS * GROUP, q_start, 0)

    tiles = 128 // math.gcd(sub, 128)
    rows_of = min(sub, 128)

    def turn(tile, _):
        value = jnp.transpose(hs_buf[:, pl.ds(pl.multiple_of(tile * 128, 128), 128)])
        block, inside = tile // (wide // 128), lax.rem(tile, wide // 128)
        c = lax.rem(block, w.nc)
        z = lax.rem(block // w.nc, w.nz)
        y = block // (w.nc * w.nz)
        if sub <= 128:
            turned[y, z, c, pl.ds(inside * tiles, tiles)] = value.reshape(tiles, rows_of, ROWS)
        else:
            per = sub // 128
            start = pl.multiple_of(lax.rem(inside, per) * 128, 128)
            turned[y, z, c, inside // per, pl.ds(start, 128), :] = value
        return _

    own_keys = k_buf.at[:, w.c, w.y, w.z]
    pltpu.make_async_copy(own_keys, own_keys, k_sem.at[0]).wait()
    pl.semaphore_wait(barrier, ns - 1 + plane - 1 + ndp - 1 + column - 1)
    key_gather.start(0, 0)
    key_gather.start(CHUNKS - 1, 0)
    hs_copy.wait()

    low, high = order_ref[2 * me], order_ref[2 * me + 1]
    line = lax.broadcasted_iota(jnp.int32, (BLK, 128), 1)
    for step in range(1, w.nc * w.ny):
        c, y = ring(w.c, step // w.ny, w.nc), ring(w.y, step % w.ny, w.ny)
        for part in range(w.nz * ROWS // BLK):
            block = order_ref[2 * ((y * w.nz + part // 2) * w.nc + c) + part % 2]
            hide = jnp.where(
                line == 0,
                jnp.where(block > low, HIDE, 0.0),
                jnp.where((line == 1) & (block > high), HIDE, 0.0),
            )
            hide_buf[step, part * BLK : part * BLK + BLK, :] = hide.astype(jnp.bfloat16)
    row = lax.broadcasted_iota(jnp.int32, (2 * ROWS, 128), 0)
    column_of = lax.rem(row, ROWS) // BLK
    lane = lax.broadcasted_iota(jnp.int32, (2 * ROWS, 128), 1)
    side_buf[...] = jnp.where(lane == column_of, 1.0, 0.0).astype(jnp.bfloat16)

    pre_buf[...] = jnp.broadcast_to(b1_ref[...], (ROWS, HIDDEN))
    per_quarter = depth // 128 // quarters
    deep = min(1024, span)
    for quarter in range(quarters):
        w1_copy(quarter).wait()

        def project(tile, _):
            at = pl.multiple_of(quarter * span + tile * deep, deep)
            pre_buf[...] += dot(hs_buf[:, pl.ds(at, deep)], w1_buf[pl.ds(at, deep), :])
            return _

        lax.fori_loop(0, span // deep, project, 0)
        lax.fori_loop(quarter * per_quarter, (quarter + 1) * per_quarter, turn, 0)
        if quarter:
            key_gather.forward(quarter - 1, 1)
        if quarter + 1 < CHUNKS - 1:
            key_gather.start(quarter + 1, 0)

    pre = pre_buf[...]
    gate = 1.0 / (1.0 + jnp.exp(-pre))
    gate_buf[...] = gate * (1.0 + pre * (1.0 - gate))
    hid_buf[...] = (pre * gate).astype(jnp.bfloat16)

    own_cols = cols.at[own_plane]

    def distance(step):
        across, along, other = step
        return (min(across, w.nx - across) + min(along, w.ny - along), across, along, other)

    steps = [
        (across, along, other)
        for across in range(w.nx)
        for along in range(w.ny)
        for other in range(w.nc)
        if across or along or other
    ]
    steps.sort(key=distance)

    def a_start(over_y):
        for across, along, other in steps:
            if (along > 0) != over_y:
                continue
            x, y, c = ring(w.x, across, w.nx), ring(w.y, along, w.ny), ring(w.c, other, w.nc)
            remote(
                turned.at[y, :, c, x], own_cols, a_send.at[0], a_recv.at[0],
                w.device(x=x, y=y, c=c),
            ).start()

    pltpu.make_async_copy(q_buf, q_buf, q_sem.at[0]).wait()
    cols[own_plane] = turned[w.y, :, w.c, w.x]

    def first_steps(step):
        if step == 1:
            key_gather.forward(CHUNKS - 1, 1)
            key_gather.forward(0, 2)
        if step == w.ny:
            key_gather.arrive(0, 2)

    def first_middle():
        key_gather.forward(1, 2)
        a_start(False)

    attend(
        0, order_ref, w, q_buf, k_buf, hide_buf, side_buf, p_buf, m_buf, mass_out, first_steps,
        first_middle,
    )

    def one_head(head, _):
        def middle():
            for other in range(1, HEADS - 1):

                @pl.when(head == other)
                def _():
                    key_gather.forward(other + 1, 2)
                    if other == 1:
                        a_start(True)

        key_gather.arrive(head, 2)
        attend(
            head, order_ref, w, q_buf, k_buf, hide_buf, side_buf, p_buf, m_buf, mass_out,
            lambda step: None, middle,
        )
        return _

    lax.fori_loop(1, HEADS, one_head, 0)

    def m_copy(hop):
        to = ring(me, hop, ns)
        return remote(mass_out.at[to], mass_in.at[hop - 1], m_send.at[0], m_recv.at[0], (dp, to))

    def m_start(hop, _):
        m_copy(hop).start()
        return _

    lax.fori_loop(1, ns, m_start, 0)
    predicted = dot_t(w2_ref[...], hid_buf[...])
    line = lax.broadcasted_iota(jnp.int32, (HEADS, ROWS), 0)
    for head in range(HEADS):
        predicted += jnp.where(line == head, b2_ref[head], 0.0)

    for chunk in range(CHUNKS):
        key_gather.drain(chunk)

    all_of(mass_in.at[pl.ds(0, ns - 1)], m_send, m_recv).wait_recv()
    mass = mass_out[me]
    for at in range(ns - 1):
        mass += mass_in[at]
    residue = predicted - jnp.log(1.0 + mass)
    out_grad = residue / length
    turned_grad = jnp.transpose(
        jnp.concatenate([out_grad, jnp.zeros((8 - HEADS, ROWS), jnp.float32)], axis=0)
    )
    w2_wide = w2_ref[...].astype(jnp.float32)
    back = turned_grad[:, 0:1] * w2_wide[0:1, :]
    for head in range(1, HEADS):
        back += turned_grad[:, head : head + 1] * w2_wide[head : head + 1, :]
    slope = back * gate_buf[...]
    s_buf[w.c, w.y, w.x] = slope.astype(jnp.bfloat16)
    for chunk in range(CHUNKS):
        slope_gather.start(chunk, 0)

    def exchange(buf, at, count, send, recv, device):
        return [
            remote(buf.at[at], buf.at[at], send.at[0], recv.at[0], device(hop))
            for hop in range(1, count)
        ]

    def z_copies():
        return exchange(
            small_z, w.z, w.nz, z_send, z_recv, lambda hop: w.device(z=ring(w.z, hop, w.nz))
        )

    def y_copies():
        return exchange(
            small_y, w.y, w.ny, y_send, y_recv, lambda hop: w.device(y=ring(w.y, hop, w.ny))
        )

    def c_copies():
        return exchange(small_c, w.c, w.nc, c_send, c_recv, lambda hop: w.device(c=1 - w.c))

    def d_copies():
        return exchange(small_d, dp, ndp, d_send, d_recv, lambda hop: (ring(dp, hop, ndp), me))

    def settle(buf, send, recv):
        if buf.shape[0] > 1:
            all_of(buf.at[pl.ds(0, buf.shape[0] - 1)], send, recv).wait_recv()
        total = buf[0]
        for at in range(1, buf.shape[0]):
            total += buf[at]
        return total

    exact = lax.Precision.HIGHEST
    second = dot(out_grad, hid_buf[...].astype(jnp.float32), exact)
    first_bias = jnp.sum(slope, axis=0, keepdims=True)
    place = lax.broadcasted_iota(jnp.int32, (1, HIDDEN), 1)
    bias_sum = jnp.sum(out_grad, axis=1, keepdims=True)
    loss = 0.5 * whole_sum(residue * residue)
    last = jnp.where(place == HEADS, loss / length, 0.0)
    for head in range(HEADS):
        last = jnp.where(place == head, bias_sum[head : head + 1, :], last)
    small_z[w.z] = jnp.concatenate(
        [second, first_bias, last, jnp.zeros((2, HIDDEN), jnp.float32)], axis=0
    )
    for copy in z_copies():
        copy.start()

    all_of(mass_in.at[pl.ds(0, ns - 1)], m_send, m_recv).wait_send()
    for chunk in range(CHUNKS):
        slope_gather.forward(chunk, 1)
    small_y[w.y] = settle(small_z, z_send, z_recv)
    for copy in y_copies():
        copy.start()
    slope_gather.forward(0, 2)
    slope_gather.forward(1, 2)

    all_of(cols.at[pl.ds(0, plane - 1)], a_send, a_recv).wait()

    def p_copy(side, hop):
        to = ring(w.z, hop, w.nz)
        return remote(
            part_buf.at[side, to], piece_buf.at[own_column],
            p_send.at[0], p_recv.at[0], w.device(z=to, l=side),
        )

    def each_piece(side, action):
        for hop in range(w.nz):
            if hop:
                action(hop)
            else:
                pl.when(w.l != side)(functools.partial(action, hop))

    for side in range(w.nl):
        chunks = range(side * CHUNKS // w.nl, (side + 1) * CHUNKS // w.nl)
        for chunk in chunks:
            if chunk >= 2:
                slope_gather.forward(chunk, 2)
        for chunk in chunks:
            slope_gather.arrive(chunk, 2)
        columns = pl.ds(side * side_width, side_width)
        total = dot(
            jnp.concatenate([cols[at].reshape(w.nz * sub, ROWS) for at in range(plane)], axis=1),
            s_buf[:, :, :, :, columns].reshape(plane * ROWS, side_width),
        )
        part_buf[side] = total.reshape(w.nz, sub, side_width)
        each_piece(side, lambda hop, side=side: p_copy(side, hop).start())
        if side == 0:
            small_c[w.c] = settle(small_y, y_send, y_recv)
            for copy in c_copies():
                copy.start()

    small_d[dp] = settle(small_c, c_send, c_recv)
    for copy in d_copies():
        copy.start()
    piece_buf[own_column] = part_buf[w.l, w.z]
    for chunk in range(CHUNKS):
        slope_gather.drain(chunk)
    for buf, send, recv in (
        (small_z, z_send, z_recv), (small_y, y_send, y_recv), (small_c, c_send, c_recv)
    ):
        if buf.shape[0] > 1:
            all_of(buf.at[pl.ds(0, buf.shape[0] - 1)], send, recv).wait_send()

    all_of(piece_buf.at[pl.ds(0, column - 1)], p_send, p_recv).wait_recv()
    piece = piece_buf[0]
    for at in range(1, column):
        piece += piece_buf[at]
    squares = piece * piece
    narrow = squares[:, 0:128]
    for at in range(1, side_width // 128):
        narrow += squares[:, at * 128 : at * 128 + 128]
    sq_seq[me] = jnp.sum(narrow, axis=0, keepdims=True)

    def e_copy(hop):
        return remote(
            sq_seq.at[me], sq_seq.at[me], e_send.at[0], e_recv.at[0], (dp, ring(me, hop, ns))
        )

    def e_start(hop, _):
        e_copy(hop).start()
        return _

    lax.fori_loop(1, ns, e_start, 0)
    full_buf[dp] = piece

    def f_copy(hop):
        own = full_buf.at[dp]
        return remote(own, own, f_send.at[0], f_recv.at[0], (ring(dp, hop, ndp), me))

    for hop in range(1, ndp):
        f_copy(hop).start()

    small = settle(small_d, d_send, d_recv)
    second = small[0:HEADS, :]
    small_ref[0:HEADS, :] = second * inverse_root(whole_sum(second * second), HEADS * HIDDEN)
    first_bias = small[4:5, :]
    small_ref[4:5, :] = first_bias * inverse_root(whole_sum(first_bias * first_bias), HIDDEN)
    small_ref[5:6, :] = small[5:6, :]
    small_ref[8 : 8 + HEADS, 0:ROWS] = mass

    all_of(piece_buf.at[pl.ds(0, column - 1)], p_send, p_recv).wait_send()
    all_of(sq_seq.at[pl.ds(0, ns - 1)], e_send, e_recv).wait_recv()
    square = sq_seq[0]
    for at in range(1, ns):
        square += sq_seq[at]
    sq_dp[dp] = square

    def g_copy(hop):
        return remote(
            sq_dp.at[dp], sq_dp.at[dp], g_send.at[0], g_recv.at[0], (ring(dp, hop, ndp), me)
        )

    for hop in range(1, ndp):
        g_copy(hop).start()
    all_of(full_buf.at[pl.ds(0, ndp - 1)], f_send, f_recv).wait_recv()
    all_of(sq_dp.at[pl.ds(0, ndp - 1)], g_send, g_recv).wait_recv()
    square = sq_dp[0]
    for at in range(1, ndp):
        square += sq_dp[at]
    scale = inverse_root(whole_sum(square), depth * HIDDEN)
    for side in range(w.nl):
        step_ref[:, side * side_width : (side + 1) * side_width] = (
            full_buf[side * w.nx : (side + 1) * w.nx].reshape(wide, side_width) * scale
        )

    all_of(sq_seq.at[pl.ds(0, ns - 1)], e_send, e_recv).wait_send()
    all_of(small_d.at[pl.ds(0, ndp - 1)], d_send, d_recv).wait_send()
    all_of(full_buf.at[pl.ds(0, ndp - 1)], f_send, f_recv).wait_send()
    all_of(sq_dp.at[pl.ds(0, ndp - 1)], g_send, g_recv).wait_send()


def finish(step_in, small_in, mass_ref, loss_ref, step_ref, second_ref, first_bias_ref, bias_ref):
    step_ref[...] = step_in[...]
    mass_ref[0] = small_in[8 : 8 + HEADS, 0:ROWS]
    loss_ref[...] = small_in[5:6, HEADS : HEADS + 1]
    second_ref[...] = small_in[0:HEADS, :]
    first_bias_ref[...] = small_in[4:5, :]
    bias_ref[...] = small_in[5:6, 0:HEADS]


def per_device(
    dp_parts, seq_parts, queries, key_rows, hidden, order, w1, b1, w2, b2
):
    f32, bf16 = jnp.float32, jnp.bfloat16
    (nl, nx), (ny, nz, nc) = dp_parts, seq_parts
    ns, ndp, plane, column = ny * nz * nc, nl * nx, nc * ny * nx, nz * nl
    depth = hidden.shape[2]
    wide = depth // ns
    sub, side_width = wide // nx, HIDDEN // nl
    vmem, smem, anywhere = (
        pl.BlockSpec(memory_space=pltpu.VMEM),
        pl.BlockSpec(memory_space=pltpu.SMEM),
        pl.BlockSpec(memory_space=pl.ANY),
    )
    dma = pltpu.SemaphoreType.DMA
    step, small = pl.pallas_call(
        functools.partial(kernel, dp_parts, seq_parts),
        out_shape=(
            jax.ShapeDtypeStruct((wide, HIDDEN), f32),
            jax.ShapeDtypeStruct((16, HIDDEN), f32),
        ),
        in_specs=[smem, smem, anywhere, anywhere, anywhere, anywhere, vmem, vmem],
        out_specs=(vmem,) * 2,
        scratch_shapes=[
            pltpu.VMEM((HEADS * GROUP * ROWS, HEAD_SIZE), bf16),
            pltpu.VMEM((HEADS, nc, ny, nz, ROWS, HEAD_SIZE), bf16),
            pltpu.VMEM((nc * ny, nz * ROWS, 128), bf16),
            pltpu.VMEM((2 * ROWS, 128), bf16),
            pltpu.VMEM((ROWS, depth), bf16),
            pltpu.VMEM((ny, nz, nc, nx, sub, ROWS), bf16),
            pltpu.VMEM((depth, HIDDEN), bf16),
            pltpu.VMEM((nc * ny, nz * ROWS, GROUP * ROWS), bf16),
            pltpu.VMEM((nc * ny, 8, GROUP * ROWS), f32),
            pltpu.VMEM((plane, nz, sub, ROWS), bf16),
            pltpu.VMEM((nc, ny, nx, ROWS, HIDDEN), bf16),
            pltpu.VMEM((ROWS, HIDDEN), f32),
            pltpu.VMEM((ROWS, HIDDEN), f32),
            pltpu.VMEM((ROWS, HIDDEN), bf16),
            pltpu.VMEM((ns, HEADS, ROWS), f32),
            pltpu.VMEM((ns, HEADS, ROWS), f32),
            pltpu.VMEM((nz, 8, HIDDEN), f32),
            pltpu.VMEM((ny, 8, HIDDEN), f32),
            pltpu.VMEM((nc, 8, HIDDEN), f32),
            pltpu.VMEM((ndp, 8, HIDDEN), f32),
            pltpu.VMEM((nl, nz, sub, side_width), f32),
            pltpu.VMEM((column, sub, side_width), f32),
            pltpu.VMEM((ndp, sub, side_width), f32),
            pltpu.VMEM((ns, 1, 128), f32),
            pltpu.VMEM((ndp, 1, 128), f32),
            dma((1,)), dma((1,)), dma((1,)), dma((CHUNKS,)),
            *[dma((CHUNKS, 3))] * 4, *[dma((1,))] * 20,
        ],
        compiler_params=pltpu.CompilerParams(
            collective_id=0, has_side_effects=True, vmem_limit_bytes=60 * 1024 * 1024
        ),
    )(
        order, b2, queries.reshape(ROWS, -1), key_rows.reshape(ROWS, -1),
        hidden.reshape(ROWS, depth), w1, b1.reshape(1, HIDDEN), w2,
    )
    mass, loss, step, second, first_bias, bias = pl.pallas_call(
        finish,
        out_shape=(
            jax.ShapeDtypeStruct((1, HEADS, ROWS), f32),
            jax.ShapeDtypeStruct((1, 1), f32),
            jax.ShapeDtypeStruct((wide, HIDDEN), f32),
            jax.ShapeDtypeStruct((HEADS, HIDDEN), f32),
            jax.ShapeDtypeStruct((1, HIDDEN), f32),
            jax.ShapeDtypeStruct((1, HEADS), f32),
        ),
        in_specs=[vmem, vmem],
        out_specs=(vmem,) * 6,
    )(step, small)
    return (
        mass, loss.reshape(()), step, second, first_bias.reshape(HIDDEN), bias.reshape(HEADS)
    )


def solution(mesh, dp_parts=DP_PARTS, seq_parts=SEQ_PARTS):
    in_specs = (P("dp", "seq", None),) * 3 + (P(),) * 5
    out_specs = (P("dp", None, "seq"), P(), P("seq", None), P(), P(), P())
    body = functools.partial(per_device, dp_parts, seq_parts)
    return jax.shard_map(
        body, mesh=mesh, in_specs=in_specs, out_specs=out_specs, check_vma=False
    )
```
